512 devices in a mesh: expert: 128 (over y_hi, z, x), dp: 4 (over y_lo, core).
Axes of the slice: x: 4, y: 4 (y_hi: 2, y_lo: 2; y = y_hi * 2 + y_lo), z: 16, core: 2. Of those that a mesh axis runs over, the one named last changes fastest.
Arguments:
- tokens: bfloat16 [12288, 2048], P(('expert', 'dp')), may hold values from -6 to 6
- expert_ids: int32 [12288, 8], P(('expert', 'dp')), may hold values from 0 to 127, all different within a row; in each aligned block of 24 rows (0 to 23, 24 to 47, ...) at most 2 rows name the same one
- route_weight: float32 [12288, 8], P(('expert', 'dp')), may hold values from 0.05 to 0.5
- cotangent: bfloat16 [12288, 2048], P(('expert', 'dp')), may hold values from -6 to 6
- holder: int32 [128], replicated, may hold values from 0 to 127, each once
- partner: int32 [128], replicated, may hold values from 0 to 127, as said below
- up_weight: bfloat16 [128, 2048, 768], P('expert', 'dp'), may hold values from -0.125 to 0.125
- down_weight: bfloat16 [128, 768, 2048], P('expert', None, 'dp'), may hold values from -0.21875 to 0.21875
- up_moment: bfloat16 [128, 2048, 768], P('expert', 'dp'), may hold values from -1.796875 to 1.796875
- down_moment: bfloat16 [128, 768, 2048], P('expert', None, 'dp'), may hold values from -1.796875 to 1.796875
Outputs:
- layer_out: bfloat16 [12288, 2048], P(('expert', 'dp'))
- up_moment_new: bfloat16 [128, 2048, 768], P('expert', 'dp')
- down_moment_new: bfloat16 [128, 768, 2048], P('expert', None, 'dp')
The draws below stay inside these ranges and needn't reach their ends.
Inputs may be any that keep to these rules, and one draw needn't show every extreme that they name: `expert_ids`: each token names 8 different experts; within each device's block of 24 tokens no expert is named by more than 2 tokens, a bound that some block reaches. `holder`: A permutation of the slots. partner[partner[s]] = s for every slot s, and exactly 2 * (32) slots have partner[s] != s.
All inputs are finite; a program needn't handle non-finite values.
Results may differ from the reference program's by a relative error of at most 0.022.
Values may be sent and summed in bfloat16 or wider, within the bound.
No kernel may reach another device: no remote copies, remote signals or barrier semaphores. Data moves between devices by JAX's collectives and lax.ppermute only.
A program may use at most 64 MiB of HBM per device.

```python
import math
import jax
import jax.numpy as jnp
import numpy as np
from jax import lax

D = 2048
F = 768
TOPK = 8
TOK_DEV = 24
EXPERTS = 128
CAP = 2
TOKENS = 12288
N_DP = 4


def draw_partner(key, part):
    order = jax.random.permutation(key, EXPERTS).astype(jnp.int32)
    pairs = EXPERTS // 4
    first = order[0:2 * pairs:2]
    second = order[1:2 * pairs:2]
    base = jnp.arange(EXPERTS, dtype=jnp.int32)
    return base.at[first].set(second).at[second].set(first)


def block_scale(rng, extent, split, low, largest):
    def one(axis_at, shards_of):
        heights = jax.random.uniform(jax.random.fold_in(jax.random.fold_in(rng, 6), axis_at), (shards_of,), jnp.float32, low / len(split), largest / len(split))
        return jnp.repeat(jnp.exp(heights), extent[axis_at] // shards_of).reshape((-1,) + (1,) * (len(extent) - axis_at - 1))

    gain = one(*split[0])
    for cut in split[1:]:
        gain = gain * one(*cut)
    return gain


def shared_out(own_key, own, number, rows, number_of, top, limit, skew):
    order = jax.random.permutation(own_key, number_of)
    packed, usual = shares(number_of, rows * top, limit, skew, True), shares(number_of, rows * top, limit, skew, False)
    places = jnp.arange(number_of)

    def named(lengths, turn):
        used = int((lengths > 0).sum())
        fixed = max(1, used // 4)
        shifted = fixed + (places - fixed + turn * (used - fixed)) % max(1, number_of - fixed)
        return jnp.zeros((number_of,), jnp.int32).at[order[jnp.where(places < fixed, places, shifted)]].set(jnp.asarray(lengths, jnp.int32))

    lengths = jnp.where(number % 4 == 0, named(packed, number // 4), named(usual, number - number // 4 - 1))
    mixed = jax.random.permutation(jax.random.fold_in(own, 3), number_of)
    donor, taker = mixed[0:number_of // 2 * 2:2], mixed[1:number_of // 2 * 2:2]
    margin = jnp.minimum(lengths[donor] - 1, limit - lengths[taker]) // 2
    margin = jnp.where((donor == order[0]) | (taker == order[0]) | (lengths[taker] == 0), 0, jnp.maximum(margin, 0))
    shifted = jax.random.randint(jax.random.fold_in(own, 4), (number_of // 2,), 0, 1 << 20) % (margin + 1)
    lengths = lengths.at[donor].add(-shifted).at[taker].add(shifted)
    labels = jnp.searchsorted(jnp.cumsum(lengths), jnp.arange(rows * top), side="right").astype(jnp.int32)
    grid = labels.reshape(top, rows).T
    grid = grid[jax.random.permutation(jax.random.fold_in(own, 1), rows)]
    turn = jax.random.randint(jax.random.fold_in(own, 2), (rows, 1), 0, top)
    return jnp.take_along_axis(grid, (jnp.arange(top)[None, :] + turn) % top, axis=1)


def shares(amount, total, bound, lean, full):
    loads = [(1 << 20) // math.isqrt(rank ** lean) + 1 for rank in range(1, amount + 1)]
    largest = bound if full else min(bound, max(-(-total // amount), total * loads[0] // sum(loads)))
    least = 1 if total - largest >= amount - 1 else 0
    counts, spare = [largest] + [least] * (amount - 1), total - largest - least * (amount - 1)
    while spare > 0:
        movable = [i for i in range(1, amount) if counts[i] < largest] or [i for i in range(1, amount) if counts[i] < bound]
        pool, remaining = sum([loads[i] for i in movable]), spare
        for i in movable:
            addition = min(bound - counts[i], max(1, remaining * loads[i] // pool), spare)
            counts[i] = counts[i] + addition
            spare = spare - addition
    return np.array(counts)


def normal_values(stream_key, shape, scale, bound, pieces=(), held_as=jnp.bfloat16):
    drawn = jax.random.normal(stream_key, shape, jnp.float32) * scale
    if len(pieces) > 0:
        drawn = block_scale(stream_key, shape, pieces, -0.22, 0.18) * drawn
    return jnp.clip(drawn, min=-bound, max=bound).astype(held_as)


def setup_inputs(seed: int = 0) -> dict:
    keys = jax.random.split(jax.random.key(seed), 11)
    tokens = normal_values(keys[0], (TOKENS, D), 1.0, 6.0, ((0, 512),))
    expert_ids_keys = jax.random.split(jax.random.fold_in(keys[1], 1), TOKENS // TOK_DEV)
    expert_ids_turns = jax.random.permutation(jax.random.fold_in(keys[1], 3), TOKENS // TOK_DEV)
    expert_ids = jax.vmap(lambda own, number: shared_out(jax.random.fold_in(keys[1], 2), own, number, TOK_DEV, EXPERTS, TOPK, CAP, 2))(expert_ids_keys, expert_ids_turns).reshape((TOKENS, TOPK))
    route_weight = jnp.clip(jnp.exp(math.log(0.5) - 2.3025851 * jax.random.uniform(keys[2], (TOKENS, TOPK), jnp.float32) ** block_scale(keys[2], (TOKENS, TOPK), ((0, 512),), -0.2, 0.2)), 0.05, 0.5)
    cotangent = normal_values(keys[3], (TOKENS, D), 1.0, 6.0, ((0, 512),))
    holder = jax.random.permutation(keys[4], EXPERTS).astype(jnp.int32)
    partner = draw_partner(jax.random.fold_in(keys[10], 71), 0)
    up_weight = normal_values(keys[6], (EXPERTS, D, F), D ** -0.5, 0.125, ((0, 128), (1, 4)))
    down_weight = normal_values(keys[7], (EXPERTS, F, D), F ** -0.5, 0.21875, ((0, 128), (2, 4)))
    up_moment = normal_values(keys[8], (EXPERTS, D, F), 0.3, 1.796875, ((0, 128), (1, 4)))
    down_moment = normal_values(keys[9], (EXPERTS, F, D), 0.3, 1.796875, ((0, 128), (2, 4)))
    return {"tokens": tokens, "expert_ids": expert_ids, "route_weight": route_weight, "cotangent": cotangent, "holder": holder, "partner": partner, "up_weight": up_weight, "down_weight": down_weight, "up_moment": up_moment, "down_moment": down_moment}


MOMENT_DECAY = 0.9


def silu_slope(preact):
    sigmoid_value = jax.nn.sigmoid(preact)
    return sigmoid_value * (1.0 + preact * (1.0 - sigmoid_value))


def reference(tokens, expert_ids, route_weight, cotangent, holder, partner, up_weight, down_weight, up_moment, down_moment):
    blocks = TOKENS // TOK_DEV
    per_block = TOK_DEV * TOPK
    quarter = D // N_DP
    expert_rows = expert_ids.reshape(blocks, per_block)
    experts = jnp.arange(EXPERTS, dtype=jnp.int32)
    hit_table = (expert_rows[:, :, None] == experts[None, None, :]).astype(jnp.int32)
    position = jnp.sum((jnp.cumsum(hit_table, axis=1) - 1) * hit_table, axis=2)
    block_index = jnp.arange(blocks, dtype=jnp.int32)[:, None]
    entry_index = ((expert_rows * blocks + block_index) * CAP + position).reshape(-1).astype(jnp.int32)
    token_index = (block_index * TOK_DEV + jnp.arange(per_block, dtype=jnp.int32)[None, :] // TOPK).reshape(-1).astype(jnp.int32)
    slot_span = blocks * CAP
    token_table = jnp.full((EXPERTS * slot_span,), TOKENS, dtype=jnp.int32).at[entry_index].set(token_index)
    weights = jnp.zeros((EXPERTS * slot_span,), jnp.float32).at[entry_index].set(route_weight.reshape(-1))
    padded_tokens = jnp.concatenate([tokens, jnp.zeros((1, D), tokens.dtype)], axis=0)
    padded_grads = jnp.concatenate([cotangent.astype(jnp.float32), jnp.zeros((1, D), jnp.float32)], axis=0)

    def one_expert(accumulated, expert):
        row_index = lax.dynamic_slice_in_dim(token_table, expert * slot_span, slot_span)
        scales = lax.dynamic_slice_in_dim(weights, expert * slot_span, slot_span)
        inputs = padded_tokens[row_index]
        cotangents = (scales[:, None] * padded_grads[row_index]).astype(jnp.bfloat16)
        old_slot = holder[expert]
        w_up = up_weight[old_slot]
        w_down = down_weight[old_slot]
        preact = jnp.zeros((slot_span, F), jnp.float32)
        back_sum = jnp.zeros((slot_span, F), jnp.float32)
        for section in range(N_DP):
            begin_at = section * quarter
            end_at = begin_at + quarter
            part_up = jnp.dot(inputs[:, begin_at:end_at], w_up[begin_at:end_at, :], preferred_element_type=jnp.float32)
            preact = preact + lax.optimization_barrier(part_up.astype(jnp.bfloat16)).astype(jnp.float32)
            part_back = jnp.dot(cotangents[:, begin_at:end_at], w_down[:, begin_at:end_at].T, preferred_element_type=jnp.float32)
            back_sum = back_sum + lax.optimization_barrier(part_back.astype(jnp.bfloat16)).astype(jnp.float32)
        hidden = jax.nn.silu(preact).astype(jnp.bfloat16)
        pre_grad = (back_sum * silu_slope(preact)).astype(jnp.bfloat16)
        outputs = jnp.dot(hidden, w_down, preferred_element_type=jnp.float32).astype(jnp.bfloat16)
        up_grad = jnp.dot(inputs.T, pre_grad, preferred_element_type=jnp.float32)
        down_grad = jnp.dot(hidden.T, cotangents, preferred_element_type=jnp.float32)
        new_up = (MOMENT_DECAY * up_moment[old_slot].astype(jnp.float32) + (1.0 - MOMENT_DECAY) * up_grad).astype(jnp.bfloat16)
        new_down = (MOMENT_DECAY * down_moment[old_slot].astype(jnp.float32) + (1.0 - MOMENT_DECAY) * down_grad).astype(jnp.bfloat16)
        accumulated = accumulated.at[row_index].add(scales[:, None] * outputs.astype(jnp.float32))
        return accumulated, (new_up, new_down)

    start = jnp.zeros((TOKENS + 1, D), jnp.float32)
    accumulated, stacked = lax.scan(one_expert, start, experts)
    inverse = jnp.zeros((EXPERTS,), jnp.int32).at[holder].set(experts)
    order = inverse[partner]
    return accumulated[:TOKENS].astype(jnp.bfloat16), stacked[0][order], stacked[1][order]
```

```python
import jax
import jax.numpy as jnp
from jax import lax
from jax.experimental import pallas as pl
from jax.experimental.pallas import tpu as pltpu
from jax.sharding import Mesh, PartitionSpec as P

MOMENT_DECAY = 0.9
AXES = ("yh", "zh", "zp", "x", "yl", "core")
SLOT_AXES = ("yh", "zh", "zp", "x")
GROUP_AXES = ("yh", "zp", "x")
DP_AXES = ("yl", "core")
BF16 = jnp.bfloat16
F32 = jnp.float32
FLIP = [(0, 1), (1, 0)]
VMEM = pl.BlockSpec(memory_space=pltpu.VMEM)
SMEM = pl.BlockSpec(memory_space=pltpu.SMEM)


def call(kernel, name, out_shape, in_specs, flops, moved):
    outs = jax.tree.map(lambda _: VMEM, out_shape)
    return pl.pallas_call(
        kernel,
        name=name,
        out_shape=out_shape,
        in_specs=in_specs,
        out_specs=outs,
        compiler_params=pltpu.CompilerParams(vmem_limit_bytes=48 * 1024 * 1024),
        cost_estimate=pl.CostEstimate(flops=flops, bytes_accessed=moved, transcendentals=0),
    )


def split3(value):
    high = value.astype(BF16)
    rest = value - high.astype(F32)
    middle = rest.astype(BF16)
    low = (rest - middle.astype(F32)).astype(BF16)
    return high, middle, low


def pack_kernel(tok_ref, cot_ref, ids_ref, weight_ref, holder_ref, out_ref):
    rows, top = ids_ref.shape
    width = tok_ref.shape[1]
    experts = holder_ref.shape[1]
    ids = ids_ref[...]
    weights = weight_ref[...]
    lane = lax.broadcasted_iota(jnp.int32, (rows, experts), 1)
    hits = [(ids[:, k : k + 1] == lane).astype(F32) for k in range(top)]
    hit = sum(hits[1:], hits[0])
    earlier = (
        lax.broadcasted_iota(jnp.int32, (rows, rows), 0)
        > lax.broadcasted_iota(jnp.int32, (rows, rows), 1)
    ).astype(F32)
    before = jnp.dot(earlier, hit, preferred_element_type=F32)
    base = 2.0 * holder_ref[...].astype(F32) + before
    high, middle, low = split3(weights)
    meta_lane = lax.broadcasted_iota(jnp.int32, (rows, 128), 1)
    meta = jnp.zeros((rows, 128), F32)
    for k in range(top):
        code = jnp.sum(hits[k] * base, axis=1, keepdims=True)
        meta = jnp.where(meta_lane == k, code, meta)
        for place, part in enumerate((high, middle, low)):
            meta = jnp.where(
                meta_lane == (place + 1) * top + k, part.astype(F32)[:, k : k + 1], meta
            )
    out_ref[:, :width] = tok_ref[...]
    out_ref[:, width : 2 * width] = cot_ref[...]
    out_ref[:, 2 * width :] = meta.astype(BF16)


def select_kernel(plane_ref, gathered_ref, out_ref, share_ref):
    total = gathered_ref.shape[0]
    targets, quarters, per_target, _ = out_ref.shape
    quarter = out_ref.shape[3] // 2
    width = quarters * quarter
    top = 8
    rows = targets * per_target
    block = total // (per_target // 2)
    plane = plane_ref[0]
    meta = gathered_ref[:, 2 * width :].astype(F32)
    row = lax.broadcasted_iota(jnp.int32, (total, rows), 1)
    token = lax.broadcasted_iota(jnp.int32, (total, rows), 0)
    target = row >> 4
    first = ((row >> 1) & 7) * block
    inside = (token >= first) & (token < first + block)
    slot = (target >> 3) * 64 + plane * 8 + (target & 7)
    wanted = jnp.where(inside, slot * 2 + (row & 1), -1).astype(F32)
    picked = jnp.zeros((total, rows), F32)
    share = jnp.zeros((total, rows), F32)
    for k in range(top):
        match = meta[:, k : k + 1] == wanted
        weight = (
            meta[:, top + k : top + k + 1]
            + meta[:, 2 * top + k : 2 * top + k + 1]
            + meta[:, 3 * top + k : 3 * top + k + 1]
        )
        picked = jnp.where(match, 1.0, picked)
        share = jnp.where(match, weight, share)
    share_ref[...] = share
    picked_t = jnp.transpose(picked).astype(BF16)
    shares_t = split3(jnp.transpose(share))
    for q in range(quarters):
        at = q * quarter
        sent = jnp.dot(
            picked_t, gathered_ref[:, at : at + quarter], preferred_element_type=F32
        ).astype(BF16)
        out_ref[:, q, :, :quarter] = sent.reshape(targets, per_target, quarter)
        cot = gathered_ref[:, width + at : width + at + quarter]
        grads = sum(jnp.dot(part, cot, preferred_element_type=F32) for part in shares_t)
        out_ref[:, q, :, quarter:] = grads.astype(BF16).reshape(targets, per_target, quarter)


def forward_kernel(me_ref, rows_ref, *refs):
    ups, downs, out_ref = refs[:4], refs[4:8], refs[8]
    targets, _, per_target, double = rows_ref.shape
    quarter = double // 2
    count = targets * per_target
    hidden_count = ups[0].shape[1]
    me = me_ref[0]
    preact = jnp.zeros((count, hidden_count), F32)
    back = jnp.zeros((count, hidden_count), F32)
    for j in range(4):
        both = rows_ref[:, me ^ j].reshape(count, double)
        preact = preact + jnp.dot(both[:, :quarter], ups[j][...], preferred_element_type=F32)
        back = back + lax.dot_general(
            both[:, quarter:],
            downs[j][...],
            (((1,), (1,)), ((), ())),
            preferred_element_type=F32,
        )
    sigmoid = 1.0 / (1.0 + jnp.exp(-preact))
    out_ref[:, :hidden_count] = (preact * sigmoid).astype(BF16)
    out_ref[:, hidden_count:] = (back * sigmoid * (1.0 + preact * (1.0 - sigmoid))).astype(BF16)


def expert_out_kernel(me_ref, acts_ref, *refs):
    downs, out_ref = refs[:4], refs[4]
    targets, _, per_target, quarter = out_ref.shape
    hidden = acts_ref[:, : downs[0].shape[0]]
    me = me_ref[0]
    for j in range(4):
        part = jnp.dot(hidden, downs[j][...], preferred_element_type=F32).astype(BF16)
        out_ref[:, me ^ j] = part.reshape(targets, per_target, quarter)


def combine_kernel(share_ref, returned_ref, out_ref):
    targets, quarters, per_target, quarter = returned_ref.shape
    shares = split3(share_ref[...])
    for q in range(quarters):
        rows = returned_ref[:, q].reshape(targets * per_target, quarter)
        mixed = sum(jnp.dot(part, rows, preferred_element_type=F32) for part in shares)
        out_ref[:, q * quarter : (q + 1) * quarter] = mixed.astype(BF16)


def moment_kernel(me_ref, rows_ref, a0, a1, a2, a3, up_ref, down_ref, out_ref):
    acts = (a0, a1, a2, a3)
    me = me_ref[0]
    features, hidden_count = up_ref.shape
    over_rows = (((0,), (0,)), ((), ()))
    up_grad = jnp.zeros((features, hidden_count), F32)
    down_grad = jnp.zeros((hidden_count, features), F32)
    for j in range(4):
        rows = rows_ref[me ^ j].reshape(acts[j].shape[0], 2 * features)
        up_grad = up_grad + lax.dot_general(
            rows[:, :features],
            acts[j][:, hidden_count:],
            over_rows,
            preferred_element_type=F32,
        )
        down_grad = down_grad + lax.dot_general(
            acts[j][:, :hidden_count],
            rows[:, features:],
            over_rows,
            preferred_element_type=F32,
        )
    rest = 1.0 - MOMENT_DECAY
    up = (MOMENT_DECAY * up_ref[...].astype(F32) + rest * up_grad).astype(BF16)
    down = (MOMENT_DECAY * down_ref[...].astype(F32) + rest * down_grad).astype(BF16)
    up = up.reshape(32, 16, hidden_count)
    for j in range(2):
        for c in range(3):
            at = j * 384 + c * 128
            out_ref[j * 32 : (j + 1) * 32, c * 16 : (c + 1) * 16, :] = up[:, :, at : at + 128]
    down = down.reshape(16, 48, features)
    for j in range(4):
        out_ref[64 + j * 16 : 80 + j * 16] = down[:, :, j * 128 : (j + 1) * 128]


def pick_kernel(partner_ref, spread_ref, out_ref):
    def step(slot, carry):
        out_ref[slot] = spread_ref[partner_ref[slot]]
        return carry

    lax.fori_loop(0, out_ref.shape[0], step, 0, unroll=8)


def unpack_kernel(pieces_ref, up_ref, down_ref):
    for j in range(2):
        for c in range(3):
            at = j * 384 + c * 128
            part = pieces_ref[j * 32 : (j + 1) * 32, c * 16 : (c + 1) * 16, :]
            up_ref[:, at : at + 128] = part.reshape(512, 128)
    for j in range(4):
        part = pieces_ref[64 + j * 16 : 80 + j * 16]
        down_ref[:, j * 128 : (j + 1) * 128] = part.reshape(768, 128)


def shape_of(dims, dtype=BF16):
    return jax.ShapeDtypeStruct(dims, dtype)


def body(
    tokens,
    expert_ids,
    route_weight,
    cotangent,
    holder,
    partner,
    up_weight,
    down_weight,
    up_moment,
    down_moment,
):
    plane = lax.axis_index("zh").reshape(1).astype(jnp.int32)
    me = lax.axis_index(DP_AXES).reshape(1).astype(jnp.int32)

    packed = call(pack_kernel, "pack", shape_of((24, 4224)), [VMEM] * 5, 10**6, 4 * 10**5)(
        tokens, cotangent, expert_ids, route_weight, holder.reshape(1, -1)
    )
    gathered = lax.all_gather(packed, "zh", axis=0, tiled=True)

    up0, down0 = up_weight[0], down_weight[0]
    up2, down2 = lax.ppermute(up0, "yl", FLIP), lax.ppermute(down0, "yl", FLIP)
    up1, down1 = lax.ppermute(up0, "core", FLIP), lax.ppermute(down0, "core", FLIP)
    up3, down3 = lax.ppermute(up2, "core", FLIP), lax.ppermute(down2, "core", FLIP)
    ups, downs = (up0, up1, up2, up3), (down0, down1, down2, down3)

    outgoing, share = call(
        select_kernel,
        "select",
        (shape_of((16, 4, 16, 1024)), shape_of((192, 256), F32)),
        [SMEM, VMEM],
        10**9,
        4 * 10**6,
    )(plane, gathered)
    rows = lax.all_to_all(outgoing, GROUP_AXES, split_axis=0, concat_axis=0, tiled=True)
    by_feature = lax.all_to_all(
        rows.transpose(1, 0, 2, 3), DP_AXES, split_axis=0, concat_axis=0, tiled=True
    )

    acts = call(
        forward_kernel,
        "forward",
        shape_of((256, 1536)),
        [SMEM] + [VMEM] * 9,
        16 * 10**8,
        9 * 10**6,
    )(me, rows, *ups, *downs)
    acts2 = lax.ppermute(acts, "yl", FLIP)
    acts1 = lax.ppermute(acts, "core", FLIP)
    acts3 = lax.ppermute(acts2, "core", FLIP)

    expert_out = call(
        expert_out_kernel,
        "expert_out",
        shape_of((16, 4, 16, 512)),
        [SMEM] + [VMEM] * 5,
        8 * 10**8,
        5 * 10**6,
    )(me, acts, *downs)

    pieces = call(
        moment_kernel,
        "moments",
        shape_of((128, 48, 128)),
        [SMEM] + [VMEM] * 7,
        32 * 10**8,
        9 * 10**6,
    )(me, by_feature, acts, acts1, acts2, acts3, up_moment[0], down_moment[0])

    returned = lax.all_to_all(expert_out, GROUP_AXES, split_axis=0, concat_axis=0, tiled=True)
    partial = call(
        combine_kernel, "combine", shape_of((192, 2048)), [VMEM, VMEM], 6 * 10**8, 2 * 10**6
    )(share, returned)
    layer_out = lax.psum_scatter(partial, "zh", scatter_dimension=0, tiled=True)

    spread = lax.all_to_all(pieces, SLOT_AXES, split_axis=0, concat_axis=0, tiled=True)
    chosen = call(
        pick_kernel, "pick", shape_of((128, 48, 128)), [SMEM, VMEM], 0, 3 * 10**6
    )(partner, spread)
    landed = lax.all_to_all(chosen, SLOT_AXES, split_axis=0, concat_axis=0, tiled=True)
    new_up, new_down = call(
        unpack_kernel,
        "unpack",
        (shape_of((512, 768)), shape_of((768, 512))),
        [VMEM],
        0,
        3 * 10**6,
    )(landed)
    return layer_out, new_up[None], new_down[None]


def solution(mesh):
    wide = Mesh(mesh.devices.reshape(2, 8, 2, 4, 2, 2), AXES)
    return jax.shard_map(
        body,
        mesh=wide,
        in_specs=(
            P(AXES, None),
            P(AXES, None),
            P(AXES, None),
            P(AXES, None),
            P(),
            P(),
            P(SLOT_AXES, DP_AXES, None),
            P(SLOT_AXES, None, DP_AXES),
            P(SLOT_AXES, DP_AXES, None),
            P(SLOT_AXES, None, DP_AXES),
        ),
        out_specs=(
            P(AXES, None),
            P(SLOT_AXES, DP_AXES, None),
            P(SLOT_AXES, None, DP_AXES),
        ),
        check_vma=False,
    )
```

```python
import jax
import jax.numpy as jnp
from jax import lax
from jax.experimental import pallas as pl
from jax.experimental.pallas import tpu as pltpu
from jax.sharding import Mesh, PartitionSpec as P

MOMENT_DECAY = 0.9
AXES = ("yh", "zh", "zp", "x", "yl", "core")
SLOT_AXES = ("yh", "zh", "zp", "x")
GROUP_AXES = ("yh", "zp", "x")
DP_AXES = ("yl", "core")
BF16 = jnp.bfloat16
F32 = jnp.float32
FLIP = [(0, 1), (1, 0)]
VMEM = pl.BlockSpec(memory_space=pltpu.VMEM)
SMEM = pl.BlockSpec(memory_space=pltpu.SMEM)
HBM = pl.BlockSpec(memory_space=pltpu.HBM)


def call(kernel, name, out_shape, in_specs, flops, moved, scratch=()):
    outs = jax.tree.map(lambda _: VMEM, out_shape)
    return pl.pallas_call(
        kernel,
        name=name,
        out_shape=out_shape,
        in_specs=in_specs,
        out_specs=outs,
        scratch_shapes=scratch,
        compiler_params=pltpu.CompilerParams(vmem_limit_bytes=62 * 1024 * 1024),
        cost_estimate=pl.CostEstimate(flops=flops, bytes_accessed=moved, transcendentals=0),
    )


def split3(value):
    high = value.astype(BF16)
    rest = value - high.astype(F32)
    middle = rest.astype(BF16)
    low = (rest - middle.astype(F32)).astype(BF16)
    return high, middle, low


def fetch(pairs, sems):
    copies = [
        pltpu.make_async_copy(source, target, sems.at[i]) for i, (source, target) in enumerate(pairs)
    ]
    for copy in copies:
        copy.start()
    return copies


def pack_kernel(tok_ref, cot_ref, ids_ref, weight_ref, holder_ref, out_ref):
    top, rows = ids_ref.shape
    width = tok_ref.shape[1]
    experts = holder_ref.shape[1]
    row_at = lax.broadcasted_iota(jnp.int32, (rows, rows), 0)
    column_at = lax.broadcasted_iota(jnp.int32, (rows, rows), 1)
    same = (row_at == column_at).astype(BF16)

    def turned(value):
        return lax.dot_general(
            same, value.astype(BF16), (((1,), (1,)), ((), ())), preferred_element_type=F32
        )

    ids = turned(ids_ref[...].astype(F32))
    parts = [turned(part) for part in split3(weight_ref[...])]
    lane = lax.broadcasted_iota(jnp.int32, (rows, experts), 1).astype(F32)
    hits = [(ids[:, k : k + 1] == lane).astype(F32) for k in range(top)]
    hit = sum(hits[1:], hits[0])
    earlier = (row_at > column_at).astype(BF16)
    before = jnp.dot(earlier, hit.astype(BF16), preferred_element_type=F32)
    base = 2.0 * holder_ref[...].astype(F32) + before
    meta_lane = lax.broadcasted_iota(jnp.int32, (rows, 128), 1)
    meta = jnp.zeros((rows, 128), F32)
    for k in range(top):
        code = jnp.sum(hits[k] * base, axis=1, keepdims=True)
        meta = jnp.where(meta_lane == k, code, meta)
        for place, part in enumerate(parts):
            meta = jnp.where(meta_lane == (place + 1) * top + k, part[:, k : k + 1], meta)
    out_ref[:, :width] = tok_ref[...]
    out_ref[:, width : 2 * width] = cot_ref[...]
    out_ref[:, 2 * width :] = meta.astype(BF16)


def select_kernel(plane_ref, gathered_ref, out_ref, share_ref):
    total = gathered_ref.shape[0]
    targets, quarters, per_target, _ = out_ref.shape
    quarter = out_ref.shape[3] // 2
    width = quarters * quarter
    top = 8
    rows = targets * per_target
    block = total // (per_target // 2)
    plane = plane_ref[0]
    meta = gathered_ref[:, 2 * width :].astype(F32)
    row = lax.broadcasted_iota(jnp.int32, (total, rows), 1)
    token = lax.broadcasted_iota(jnp.int32, (total, rows), 0)
    target = row >> 4
    first = ((row >> 1) & 7) * block
    inside = (token >= first) & (token < first + block)
    slot = (target >> 3) * 64 + plane * 8 + (target & 7)
    wanted = jnp.where(inside, slot * 2 + (row & 1), -1).astype(F32)
    picked = jnp.zeros((total, rows), F32)
    share = jnp.zeros((total, rows), F32)
    for k in range(top):
        match = meta[:, k : k + 1] == wanted
        weight = (
            meta[:, top + k : top + k + 1]
            + meta[:, 2 * top + k : 2 * top + k + 1]
            + meta[:, 3 * top + k : 3 * top + k + 1]
        )
        picked = jnp.where(match, 1.0, picked)
        share = jnp.where(match, weight, share)
    share_ref[...] = share
    picked_t = jnp.transpose(picked).astype(BF16)
    shares_t = split3(jnp.transpose(share))
    for q in range(quarters):
        at = q * quarter
        sent = jnp.dot(
            picked_t, gathered_ref[:, at : at + quarter], preferred_element_type=F32
        ).astype(BF16)
        out_ref[:, q, :, :quarter] = sent.reshape(targets, per_target, quarter)
        cot = gathered_ref[:, width + at : width + at + quarter]
        grads = sum(jnp.dot(part, cot, preferred_element_type=F32) for part in shares_t)
        out_ref[:, q, :, quarter:] = grads.astype(BF16).reshape(targets, per_target, quarter)


def forward_kernel(me_ref, rows_ref, *refs):
    sources, out_ref, ups, downs, sems = refs[:8], refs[8], refs[9], refs[10], refs[11]
    copies = fetch(
        [(sources[j + 4 * kind], held.at[j]) for j in range(4) for kind, held in ((0, ups), (1, downs))],
        sems,
    )
    targets, _, per_target, double = rows_ref.shape
    quarter = double // 2
    count = targets * per_target
    hidden_count = ups.shape[2]
    me = me_ref[0]
    preact = jnp.zeros((count, hidden_count), F32)
    back = jnp.zeros((count, hidden_count), F32)
    for j in range(4):
        both = rows_ref[:, me ^ j].reshape(count, double)
        copies[2 * j].wait()
        preact = preact + jnp.dot(both[:, :quarter], ups[j], preferred_element_type=F32)
        copies[2 * j + 1].wait()
        back = back + lax.dot_general(
            both[:, quarter:], downs[j], (((1,), (1,)), ((), ())), preferred_element_type=F32
        )
    sigmoid = 1.0 / (1.0 + jnp.exp(-preact))
    out_ref[:, :hidden_count] = (preact * sigmoid).astype(BF16)
    out_ref[:, hidden_count:] = (back * sigmoid * (1.0 + preact * (1.0 - sigmoid))).astype(BF16)


def expert_out_kernel(me_ref, acts_ref, *refs):
    sources, out_ref, downs, sems = refs[:4], refs[4], refs[5], refs[6]
    copies = fetch([(sources[j], downs.at[j]) for j in range(4)], sems)
    targets, _, per_target, quarter = out_ref.shape
    hidden = acts_ref[:, : downs.shape[1]]
    me = me_ref[0]
    for j in range(4):
        copies[j].wait()
        part = jnp.dot(hidden, downs[j], preferred_element_type=F32).astype(BF16)
        out_ref[:, me ^ j] = part.reshape(targets, per_target, quarter)


def combine_kernel(share_ref, returned_ref, out_ref):
    targets, quarters, per_target, quarter = returned_ref.shape
    shares = split3(share_ref[...])
    for q in range(quarters):
        rows = returned_ref[:, q].reshape(targets * per_target, quarter)
        mixed = sum(jnp.dot(part, rows, preferred_element_type=F32) for part in shares)
        out_ref[:, q * quarter : (q + 1) * quarter] = mixed.astype(BF16)


def moment_kernel(
    me_ref, rows_ref, a0, a1, a2, a3, up_hbm, down_hbm, out_ref, up_ref, down_ref, sems
):
    copies = fetch([(up_hbm, up_ref), (down_hbm, down_ref)], sems)
    acts = (a0, a1, a2, a3)
    me = me_ref[0]
    features, hidden_count = up_ref.shape
    over_rows = (((0,), (0,)), ((), ()))
    up_grad = jnp.zeros((features, hidden_count), F32)
    down_grad = jnp.zeros((hidden_count, features), F32)
    for j in range(4):
        rows = rows_ref[me ^ j].reshape(acts[j].shape[0], 2 * features)
        up_grad = up_grad + lax.dot_general(
            rows[:, :features],
            acts[j][:, hidden_count:],
            over_rows,
            preferred_element_type=F32,
        )
        down_grad = down_grad + lax.dot_general(
            acts[j][:, :hidden_count],
            rows[:, features:],
            over_rows,
            preferred_element_type=F32,
        )
    rest = 1.0 - MOMENT_DECAY
    for copy in copies:
        copy.wait()
    up = (MOMENT_DECAY * up_ref[...].astype(F32) + rest * up_grad).astype(BF16)
    down = (MOMENT_DECAY * down_ref[...].astype(F32) + rest * down_grad).astype(BF16)
    up = up.reshape(32, 16, hidden_count)
    for j in range(2):
        for c in range(3):
            at = j * 384 + c * 128
            out_ref[j * 32 : (j + 1) * 32, c * 16 : (c + 1) * 16, :] = up[:, :, at : at + 128]
    down = down.reshape(16, 48, features)
    for j in range(4):
        out_ref[64 + j * 16 : 80 + j * 16] = down[:, :, j * 128 : (j + 1) * 128]


def pick_kernel(partner_ref, spread_ref, out_ref):
    def step(slot, carry):
        out_ref[slot] = spread_ref[partner_ref[slot]]
        return carry

    lax.fori_loop(0, out_ref.shape[0], step, 0, unroll=8)


def unpack_kernel(pieces_ref, up_ref, down_ref):
    for j in range(2):
        for c in range(3):
            at = j * 384 + c * 128
            part = pieces_ref[j * 32 : (j + 1) * 32, c * 16 : (c + 1) * 16, :]
            up_ref[:, at : at + 128] = part.reshape(512, 128)
    for j in range(4):
        part = pieces_ref[64 + j * 16 : 80 + j * 16]
        down_ref[:, j * 128 : (j + 1) * 128] = part.reshape(768, 128)


def shape_of(dims, dtype=BF16):
    return jax.ShapeDtypeStruct(dims, dtype)


def body(
    tokens,
    expert_ids,
    route_weight,
    cotangent,
    holder,
    partner,
    up_weight,
    down_weight,
    up_moment,
    down_moment,
):
    plane = lax.axis_index("zh").reshape(1).astype(jnp.int32)
    me = lax.axis_index(DP_AXES).reshape(1).astype(jnp.int32)

    packed = call(pack_kernel, "pack", shape_of((24, 4224)), [VMEM] * 5, 10**6, 4 * 10**5)(
        tokens, cotangent, expert_ids.T, route_weight.T, holder.reshape(1, -1)
    )
    gathered = lax.all_gather(packed, "zh", axis=0, tiled=True)

    up0, down0 = up_weight[0], down_weight[0]
    up2, down2 = lax.ppermute(up0, "yl", FLIP), lax.ppermute(down0, "yl", FLIP)
    up1, down1 = lax.ppermute(up0, "core", FLIP), lax.ppermute(down0, "core", FLIP)
    up3, down3 = lax.ppermute(up2, "core", FLIP), lax.ppermute(down2, "core", FLIP)
    gathered, up1, up2, up3, down1, down2, down3 = lax.optimization_barrier(
        (gathered, up1, up2, up3, down1, down2, down3)
    )
    ups, downs = (up0, up1, up2, up3), (down0, down1, down2, down3)

    outgoing, share = call(
        select_kernel,
        "select",
        (shape_of((16, 4, 16, 1024)), shape_of((192, 256), F32)),
        [SMEM, VMEM],
        10**9,
        4 * 10**6,
    )(plane, gathered)
    rows = lax.all_to_all(outgoing, GROUP_AXES, split_axis=0, concat_axis=0, tiled=True)
    by_feature = lax.all_to_all(
        rows.transpose(1, 0, 2, 3), DP_AXES, split_axis=0, concat_axis=0, tiled=True
    )

    acts = call(
        forward_kernel,
        "forward",
        shape_of((256, 1536)),
        [SMEM, VMEM] + [HBM] * 8,
        16 * 10**8,
        9 * 10**6,
        (
            pltpu.VMEM((4, 512, 768), BF16),
            pltpu.VMEM((4, 768, 512), BF16),
            pltpu.SemaphoreType.DMA((8,)),
        ),
    )(me, rows, *ups, *downs)
    acts2 = lax.ppermute(acts, "yl", FLIP)
    acts1 = lax.ppermute(acts, "core", FLIP)

    expert_out = call(
        expert_out_kernel,
        "expert_out",
        shape_of((16, 4, 16, 512)),
        [SMEM, VMEM] + [HBM] * 4,
        8 * 10**8,
        5 * 10**6,
        (pltpu.VMEM((4, 768, 512), BF16), pltpu.SemaphoreType.DMA((4,))),
    )(me, acts, *downs)

    by_feature, acts2, expert_out = lax.optimization_barrier((by_feature, acts2, expert_out))
    acts3 = lax.ppermute(acts2, "core", FLIP)
    returned = lax.all_to_all(expert_out, GROUP_AXES, split_axis=0, concat_axis=0, tiled=True)
    partial = call(
        combine_kernel, "combine", shape_of((192, 2048)), [VMEM, VMEM], 6 * 10**8, 2 * 10**6
    )(share, returned)
    pieces = call(
        moment_kernel,
        "moments",
        shape_of((128, 48, 128)),
        [SMEM] + [VMEM] * 5 + [HBM] * 2,
        32 * 10**8,
        9 * 10**6,
        (
            pltpu.VMEM((512, 768), BF16),
            pltpu.VMEM((768, 512), BF16),
            pltpu.SemaphoreType.DMA((2,)),
        ),
    )(me, by_feature, acts, acts1, acts2, acts3, up_moment[0], down_moment[0])

    partial, pieces = lax.optimization_barrier((partial, pieces))
    layer_out = lax.psum_scatter(partial, "zh", scatter_dimension=0, tiled=True)

    spread = lax.all_to_all(pieces, SLOT_AXES, split_axis=0, concat_axis=0, tiled=True)
    chosen = call(
        pick_kernel, "pick", shape_of((128, 48, 128)), [SMEM, VMEM], 0, 3 * 10**6
    )(partner, spread)
    landed = lax.all_to_all(chosen, SLOT_AXES, split_axis=0, concat_axis=0, tiled=True)
    new_up, new_down = call(
        unpack_kernel,
        "unpack",
        (shape_of((512, 768)), shape_of((768, 512))),
        [VMEM],
        0,
        3 * 10**6,
    )(landed)
    return layer_out, new_up[None], new_down[None]


def solution(mesh):
    wide = Mesh(mesh.devices.reshape(2, 8, 2, 4, 2, 2), AXES)
    return jax.shard_map(
        body,
        mesh=wide,
        in_specs=(
            P(AXES, None),
            P(AXES, None),
            P(AXES, None),
            P(AXES, None),
            P(),
            P(),
            P(SLOT_AXES, DP_AXES, None),
            P(SLOT_AXES, None, DP_AXES),
            P(SLOT_AXES, DP_AXES, None),
            P(SLOT_AXES, None, DP_AXES),
        ),
        out_specs=(
            P(AXES, None),
            P(SLOT_AXES, DP_AXES, None),
            P(SLOT_AXES, None, DP_AXES),
        ),
        check_vma=False,
    )
```

```python
import jax
import jax.numpy as jnp
from jax import lax
from jax.experimental import pallas as pl
from jax.experimental.pallas import tpu as pltpu
from jax.sharding import Mesh, PartitionSpec as P

MOMENT_DECAY = 0.9
AXES = ("yh", "zh", "zp", "x", "yl", "core")
SLOT_AXES = ("yh", "zh", "zp", "x")
GROUP_AXES = ("yh", "zp", "x")
DP_AXES = ("yl", "core")
BF16 = jnp.bfloat16
F32 = jnp.float32
FLIP = [(0, 1), (1, 0)]
VMEM = pl.BlockSpec(memory_space=pltpu.VMEM)
SMEM = pl.BlockSpec(memory_space=pltpu.SMEM)
HBM = pl.BlockSpec(memory_space=pltpu.HBM)


def call(kernel, name, out_shape, in_specs, flops, moved, scratch=(), grant=62):
    outs = jax.tree.map(lambda _: VMEM, out_shape)
    return pl.pallas_call(
        kernel,
        name=name,
        out_shape=out_shape,
        in_specs=in_specs,
        out_specs=outs,
        scratch_shapes=scratch,
        compiler_params=pltpu.CompilerParams(vmem_limit_bytes=grant * 1024 * 1024),
        cost_estimate=pl.CostEstimate(flops=flops, bytes_accessed=moved, transcendentals=0),
    )


def split3(value):
    high = value.astype(BF16)
    rest = value - high.astype(F32)
    middle = rest.astype(BF16)
    low = (rest - middle.astype(F32)).astype(BF16)
    return high, middle, low


def fetch(pairs, sems):
    copies = [
        pltpu.make_async_copy(source, target, sems.at[i]) for i, (source, target) in enumerate(pairs)
    ]
    for copy in copies:
        copy.start()
    return copies


def pack_kernel(tok_ref, cot_ref, ids_ref, weight_ref, holder_ref, out_ref):
    top, rows = ids_ref.shape
    width = tok_ref.shape[1]
    experts = holder_ref.shape[1]
    row_at = lax.broadcasted_iota(jnp.int32, (rows, rows), 0)
    column_at = lax.broadcasted_iota(jnp.int32, (rows, rows), 1)
    same = (row_at == column_at).astype(BF16)

    def turned(value):
        return lax.dot_general(
            same, value.astype(BF16), (((1,), (1,)), ((), ())), preferred_element_type=F32
        )

    ids = turned(ids_ref[...].astype(F32))
    parts = [turned(part) for part in split3(weight_ref[...])]
    lane = lax.broadcasted_iota(jnp.int32, (rows, experts), 1).astype(F32)
    hits = [(ids[:, k : k + 1] == lane).astype(F32) for k in range(top)]
    hit = sum(hits[1:], hits[0])
    earlier = (row_at > column_at).astype(BF16)
    before = jnp.dot(earlier, hit.astype(BF16), preferred_element_type=F32)
    base = 2.0 * holder_ref[...].astype(F32) + before
    meta_lane = lax.broadcasted_iota(jnp.int32, (rows, 128), 1)
    meta = jnp.zeros((rows, 128), F32)
    for k in range(top):
        code = jnp.sum(hits[k] * base, axis=1, keepdims=True)
        meta = jnp.where(meta_lane == k, code, meta)
        for place, part in enumerate(parts):
            meta = jnp.where(meta_lane == (place + 1) * top + k, part[:, k : k + 1], meta)
    out_ref[:, :width] = tok_ref[...]
    out_ref[:, width : 2 * width] = cot_ref[...]
    out_ref[:, 2 * width :] = meta.astype(BF16)


def select_kernel(plane_ref, gathered_ref, out_ref, share_ref):
    total = gathered_ref.shape[0]
    targets, quarters, per_target, _ = out_ref.shape
    quarter = out_ref.shape[3] // 2
    width = quarters * quarter
    top = 8
    rows = targets * per_target
    block = total // (per_target // 2)
    plane = plane_ref[0]
    meta = gathered_ref[:, 2 * width :].astype(F32)
    row = lax.broadcasted_iota(jnp.int32, (total, rows), 1)
    token = lax.broadcasted_iota(jnp.int32, (total, rows), 0)
    target = row >> 4
    first = ((row >> 1) & 7) * block
    inside = (token >= first) & (token < first + block)
    slot = (target >> 3) * 64 + plane * 8 + (target & 7)
    wanted = jnp.where(inside, slot * 2 + (row & 1), -1).astype(F32)
    picked = jnp.zeros((total, rows), F32)
    share = jnp.zeros((total, rows), F32)
    for k in range(top):
        match = meta[:, k : k + 1] == wanted
        weight = (
            meta[:, top + k : top + k + 1]
            + meta[:, 2 * top + k : 2 * top + k + 1]
            + meta[:, 3 * top + k : 3 * top + k + 1]
        )
        picked = jnp.where(match, 1.0, picked)
        share = jnp.where(match, weight, share)
    share_ref[...] = share
    picked_t = jnp.transpose(picked).astype(BF16)
    shares_t = split3(jnp.transpose(share))
    for q in range(quarters):
        at = q * quarter
        sent = jnp.dot(
            picked_t, gathered_ref[:, at : at + quarter], preferred_element_type=F32
        ).astype(BF16)
        out_ref[:, q, :, :quarter] = sent.reshape(targets, per_target, quarter)
        cot = gathered_ref[:, width + at : width + at + quarter]
        grads = sum(jnp.dot(part, cot, preferred_element_type=F32) for part in shares_t)
        out_ref[:, q, :, quarter:] = grads.astype(BF16).reshape(targets, per_target, quarter)


def forward_kernel(me_ref, rows_ref, *refs):
    sources, out_ref, ups, downs, sems = refs[:8], refs[8], refs[9], refs[10], refs[11]
    copies = fetch(
        [(sources[j + 4 * kind], held.at[j]) for j in range(4) for kind, held in ((0, ups), (1, downs))],
        sems,
    )
    targets, _, per_target, double = rows_ref.shape
    quarter = double // 2
    count = targets * per_target
    hidden_count = ups.shape[2]
    me = me_ref[0]
    preact = jnp.zeros((count, hidden_count), F32)
    back = jnp.zeros((count, hidden_count), F32)
    for j in range(4):
        both = rows_ref[:, me ^ j].reshape(count, double)
        copies[2 * j].wait()
        preact = preact + jnp.dot(both[:, :quarter], ups[j], preferred_element_type=F32)
        copies[2 * j + 1].wait()
        back = back + lax.dot_general(
            both[:, quarter:], downs[j], (((1,), (1,)), ((), ())), preferred_element_type=F32
        )
    sigmoid = 1.0 / (1.0 + jnp.exp(-preact))
    out_ref[:, :hidden_count] = (preact * sigmoid).astype(BF16)
    out_ref[:, hidden_count:] = (back * sigmoid * (1.0 + preact * (1.0 - sigmoid))).astype(BF16)


def expert_out_kernel(me_ref, column_ref, acts_ref, *refs):
    sources, outs = refs[:4], refs[4:20]
    downs, rows, sems = refs[20:]
    copies = fetch([(sources[j], downs.at[j]) for j in range(4)], sems)
    targets, _, per_target, quarter = rows.shape
    hidden = acts_ref[:, : downs.shape[1]]
    me, column = me_ref[0], column_ref[0]
    for j in range(4):
        copies[j].wait()
        part = jnp.dot(hidden, downs[j], preferred_element_type=F32).astype(BF16)
        rows[:, me ^ j] = part.reshape(targets, per_target, quarter)
    for r in range(targets):
        outs[r][...] = rows[column ^ r]


def combine_kernel(column_ref, share_ref, *refs):
    returned, out_ref, rows = refs[:16], refs[16], refs[17]
    targets, quarters, per_target, quarter = rows.shape
    column = column_ref[0]
    for r in range(targets):
        rows[column ^ r] = returned[r][...]
    shares = split3(share_ref[...])
    for q in range(quarters):
        part = rows[:, q].reshape(targets * per_target, quarter)
        mixed = sum(jnp.dot(share, part, preferred_element_type=F32) for share in shares)
        out_ref[:, q * quarter : (q + 1) * quarter] = mixed.astype(BF16)


def moment_kernel(
    me_ref, rows_ref, a0, a1, a2, a3, up_hbm, down_hbm, out_ref, up_ref, down_ref, sems
):
    copies = fetch([(up_hbm, up_ref), (down_hbm, down_ref)], sems)
    acts = (a0, a1, a2, a3)
    me = me_ref[0]
    features, hidden_count = up_ref.shape
    over_rows = (((0,), (0,)), ((), ()))
    up_grad = jnp.zeros((features, hidden_count), F32)
    down_grad = jnp.zeros((hidden_count, features), F32)
    for j in range(4):
        rows = rows_ref[me ^ j].reshape(acts[j].shape[0], 2 * features)
        up_grad = up_grad + lax.dot_general(
            rows[:, :features],
            acts[j][:, hidden_count:],
            over_rows,
            preferred_element_type=F32,
        )
        down_grad = down_grad + lax.dot_general(
            acts[j][:, :hidden_count],
            rows[:, features:],
            over_rows,
            preferred_element_type=F32,
        )
    rest = 1.0 - MOMENT_DECAY
    for copy in copies:
        copy.wait()
    up = (MOMENT_DECAY * up_ref[...].astype(F32) + rest * up_grad).astype(BF16)
    down = (MOMENT_DECAY * down_ref[...].astype(F32) + rest * down_grad).astype(BF16)
    up = up.reshape(32, 16, hidden_count)
    for j in range(2):
        for c in range(3):
            at = j * 384 + c * 128
            out_ref[j * 32 : (j + 1) * 32, c * 16 : (c + 1) * 16, :] = up[:, :, at : at + 128]
    down = down.reshape(16, 48, features)
    for j in range(4):
        out_ref[64 + j * 16 : 80 + j * 16] = down[:, :, j * 128 : (j + 1) * 128]


def pick_kernel(partner_ref, spread_ref, out_ref):
    def step(slot, carry):
        out_ref[slot] = spread_ref[partner_ref[slot]]
        return carry

    lax.fori_loop(0, out_ref.shape[0], step, 0, unroll=8)


def unpack_kernel(pieces_ref, up_ref, down_ref):
    for j in range(2):
        for c in range(3):
            at = j * 384 + c * 128
            part = pieces_ref[j * 32 : (j + 1) * 32, c * 16 : (c + 1) * 16, :]
            up_ref[:, at : at + 128] = part.reshape(512, 128)
    for j in range(4):
        part = pieces_ref[64 + j * 16 : 80 + j * 16]
        down_ref[:, j * 128 : (j + 1) * 128] = part.reshape(768, 128)


def shape_of(dims, dtype=BF16):
    return jax.ShapeDtypeStruct(dims, dtype)


def body(
    tokens,
    expert_ids,
    route_weight,
    cotangent,
    holder,
    partner,
    up_weight,
    down_weight,
    up_moment,
    down_moment,
):
    plane = lax.axis_index("zh").reshape(1).astype(jnp.int32)
    me = lax.axis_index(DP_AXES).reshape(1).astype(jnp.int32)
    column = lax.axis_index(GROUP_AXES).reshape(1).astype(jnp.int32)

    packed = call(pack_kernel, "pack", shape_of((24, 4224)), [VMEM] * 5, 10**6, 4 * 10**5)(
        tokens, cotangent, expert_ids.T, route_weight.T, holder.reshape(1, -1)
    )
    gathered = lax.all_gather(packed, "zh", axis=0, tiled=True)

    up0, down0 = up_weight[0], down_weight[0]
    up2, down2 = lax.ppermute(up0, "yl", FLIP), lax.ppermute(down0, "yl", FLIP)
    up1, down1 = lax.ppermute(up0, "core", FLIP), lax.ppermute(down0, "core", FLIP)
    up3, down3 = lax.ppermute(up2, "core", FLIP), lax.ppermute(down2, "core", FLIP)
    gathered, up1, up2, up3, down1, down2, down3 = lax.optimization_barrier(
        (gathered, up1, up2, up3, down1, down2, down3)
    )
    ups, downs = (up0, up1, up2, up3), (down0, down1, down2, down3)

    outgoing, share = call(
        select_kernel,
        "select",
        (shape_of((16, 4, 16, 1024)), shape_of((192, 256), F32)),
        [SMEM, VMEM],
        10**9,
        4 * 10**6,
    )(plane, gathered)
    rows = lax.all_to_all(outgoing, GROUP_AXES, split_axis=0, concat_axis=0, tiled=True)
    by_feature = lax.all_to_all(
        rows.transpose(1, 0, 2, 3), DP_AXES, split_axis=0, concat_axis=0, tiled=True
    )

    acts = call(
        forward_kernel,
        "forward",
        shape_of((256, 1536)),
        [SMEM, VMEM] + [HBM] * 8,
        16 * 10**8,
        9 * 10**6,
        (
            pltpu.VMEM((4, 512, 768), BF16),
            pltpu.VMEM((4, 768, 512), BF16),
            pltpu.SemaphoreType.DMA((8,)),
        ),
    )(me, rows, *ups, *downs)
    acts2 = lax.ppermute(acts, "yl", FLIP)
    acts1 = lax.ppermute(acts, "core", FLIP)
    expert_out = call(
        expert_out_kernel,
        "expert_out",
        [shape_of((4, 16, 512))] * 16,
        [SMEM, SMEM, VMEM] + [HBM] * 4,
        8 * 10**8,
        5 * 10**6,
        (
            pltpu.VMEM((4, 768, 512), BF16),
            pltpu.VMEM((16, 4, 16, 512), BF16),
            pltpu.SemaphoreType.DMA((4,)),
        ),
    )(me, column, acts, *downs)
    by_feature, acts1, acts2, expert_out = lax.optimization_barrier(
        (by_feature, acts1, acts2, expert_out)
    )
    acts3 = lax.ppermute(acts2, "core", FLIP)

    pieces = call(
        moment_kernel,
        "moments",
        shape_of((128, 48, 128)),
        [SMEM] + [VMEM] * 5 + [HBM] * 2,
        32 * 10**8,
        9 * 10**6,
        (
            pltpu.VMEM((512, 768), BF16),
            pltpu.VMEM((768, 512), BF16),
            pltpu.SemaphoreType.DMA((2,)),
        ),
    )(me, by_feature, acts, acts1, acts2, acts3, up_moment[0], down_moment[0])

    spread = lax.all_to_all(pieces, SLOT_AXES, split_axis=0, concat_axis=0, tiled=True)

    _, expert_out = lax.optimization_barrier((pieces, expert_out))
    returned = [expert_out[0]] + [
        lax.ppermute(expert_out[r], GROUP_AXES, [(c, c ^ r) for c in range(16)])
        for r in range(1, 16)
    ]
    partial = call(
        combine_kernel,
        "combine",
        shape_of((192, 2048)),
        [SMEM, VMEM] + [VMEM] * 16,
        6 * 10**8,
        2 * 10**6,
        (pltpu.VMEM((16, 4, 16, 512), BF16),),
        16,
    )(column, share, *returned)
    spread, partial = lax.optimization_barrier((spread, partial))
    layer_out = lax.psum_scatter(partial, "zh", scatter_dimension=0, tiled=True)

    chosen = call(
        pick_kernel, "pick", shape_of((128, 48, 128)), [SMEM, VMEM], 0, 3 * 10**6, (), 12
    )(partner, spread)
    landed = lax.all_to_all(chosen, SLOT_AXES, split_axis=0, concat_axis=0, tiled=True)
    new_up, new_down = call(
        unpack_kernel,
        "unpack",
        (shape_of((512, 768)), shape_of((768, 512))),
        [VMEM],
        0,
        3 * 10**6,
        (),
        12,
    )(landed)
    return layer_out, new_up[None], new_down[None]


def solution(mesh):
    wide = Mesh(mesh.devices.reshape(2, 8, 2, 4, 2, 2), AXES)
    return jax.shard_map(
        body,
        mesh=wide,
        in_specs=(
            P(AXES, None),
            P(AXES, None),
            P(AXES, None),
            P(AXES, None),
            P(),
            P(),
            P(SLOT_AXES, DP_AXES, None),
            P(SLOT_AXES, None, DP_AXES),
            P(SLOT_AXES, DP_AXES, None),
            P(SLOT_AXES, None, DP_AXES),
        ),
        out_specs=(
            P(AXES, None),
            P(SLOT_AXES, DP_AXES, None),
            P(SLOT_AXES, None, DP_AXES),
        ),
        check_vma=False,
    )
```

```python
import jax
import jax.numpy as jnp
from jax import lax
from jax.experimental import pallas as pl
from jax.experimental.pallas import tpu as pltpu
from jax.sharding import Mesh, PartitionSpec as P

MOMENT_DECAY = 0.9
AXES = ("yh", "zh", "zp", "x", "yl", "core")
SLOT_AXES = ("yh", "zh", "zp", "x")
GROUP_AXES = ("yh", "zp", "x")
DP_AXES = ("yl", "core")
BF16 = jnp.bfloat16
F32 = jnp.float32
FLIP = [(0, 1), (1, 0)]
VMEM = pl.BlockSpec(memory_space=pltpu.VMEM)
SMEM = pl.BlockSpec(memory_space=pltpu.SMEM)
HBM = pl.BlockSpec(memory_space=pltpu.HBM)


def call(kernel, name, out_shape, in_specs, flops, moved, scratch=(), grant=62):
    outs = jax.tree.map(lambda _: VMEM, out_shape)
    return pl.pallas_call(
        kernel,
        name=name,
        out_shape=out_shape,
        in_specs=in_specs,
        out_specs=outs,
        scratch_shapes=scratch,
        compiler_params=pltpu.CompilerParams(vmem_limit_bytes=grant * 1024 * 1024),
        cost_estimate=pl.CostEstimate(flops=flops, bytes_accessed=moved, transcendentals=0),
    )


def split3(value):
    high = value.astype(BF16)
    rest = value - high.astype(F32)
    middle = rest.astype(BF16)
    low = (rest - middle.astype(F32)).astype(BF16)
    return high, middle, low


def fetch(pairs, sems):
    copies = [
        pltpu.make_async_copy(source, target, sems.at[i]) for i, (source, target) in enumerate(pairs)
    ]
    for copy in copies:
        copy.start()
    return copies


def pack_kernel(tok_ref, cot_ref, ids_ref, weight_ref, holder_ref, out_ref):
    top, rows = ids_ref.shape
    width = tok_ref.shape[1]
    experts = holder_ref.shape[1]
    row_at = lax.broadcasted_iota(jnp.int32, (rows, rows), 0)
    column_at = lax.broadcasted_iota(jnp.int32, (rows, rows), 1)
    same = (row_at == column_at).astype(BF16)

    def turned(value):
        return lax.dot_general(
            same, value.astype(BF16), (((1,), (1,)), ((), ())), preferred_element_type=F32
        )

    ids = turned(ids_ref[...].astype(F32))
    parts = [turned(part) for part in split3(weight_ref[...])]
    lane = lax.broadcasted_iota(jnp.int32, (rows, experts), 1).astype(F32)
    hits = [(ids[:, k : k + 1] == lane).astype(F32) for k in range(top)]
    hit = sum(hits[1:], hits[0])
    earlier = (row_at > column_at).astype(BF16)
    before = jnp.dot(earlier, hit.astype(BF16), preferred_element_type=F32)
    base = 2.0 * holder_ref[...].astype(F32) + before
    meta_lane = lax.broadcasted_iota(jnp.int32, (rows, 128), 1)
    meta = jnp.zeros((rows, 128), F32)
    for k in range(top):
        code = jnp.sum(hits[k] * base, axis=1, keepdims=True)
        meta = jnp.where(meta_lane == k, code, meta)
        for place, part in enumerate(parts):
            meta = jnp.where(meta_lane == (place + 1) * top + k, part[:, k : k + 1], meta)
    out_ref[:, :width] = tok_ref[...]
    out_ref[:, width : 2 * width] = cot_ref[...]
    out_ref[:, 2 * width :] = meta.astype(BF16)


def select_kernel(plane_ref, gathered_ref, out_ref, share_ref):
    total = gathered_ref.shape[0]
    targets, quarters, per_target, _ = out_ref.shape
    quarter = out_ref.shape[3] // 2
    width = quarters * quarter
    top = 8
    rows = targets * per_target
    block = total // (per_target // 2)
    plane = plane_ref[0]
    meta = gathered_ref[:, 2 * width :].astype(F32)
    row = lax.broadcasted_iota(jnp.int32, (total, rows), 1)
    token = lax.broadcasted_iota(jnp.int32, (total, rows), 0)
    target = row >> 4
    first = ((row >> 1) & 7) * block
    inside = (token >= first) & (token < first + block)
    slot = (target >> 3) * 64 + plane * 8 + (target & 7)
    wanted = jnp.where(inside, slot * 2 + (row & 1), -1).astype(F32)
    picked = jnp.zeros((total, rows), F32)
    share = jnp.zeros((total, rows), F32)
    for k in range(top):
        match = meta[:, k : k + 1] == wanted
        weight = (
            meta[:, top + k : top + k + 1]
            + meta[:, 2 * top + k : 2 * top + k + 1]
            + meta[:, 3 * top + k : 3 * top + k + 1]
        )
        picked = jnp.where(match, 1.0, picked)
        share = jnp.where(match, weight, share)
    share_ref[...] = share
    picked_t = jnp.transpose(picked).astype(BF16)
    shares_t = split3(jnp.transpose(share))
    for q in range(quarters):
        at = q * quarter
        sent = jnp.dot(
            picked_t, gathered_ref[:, at : at + quarter], preferred_element_type=F32
        ).astype(BF16)
        out_ref[:, q, :, :quarter] = sent.reshape(targets, per_target, quarter)
        cot = gathered_ref[:, width + at : width + at + quarter]
        grads = sum(jnp.dot(part, cot, preferred_element_type=F32) for part in shares_t)
        out_ref[:, q, :, quarter:] = grads.astype(BF16).reshape(targets, per_target, quarter)


def forward_kernel(me_ref, rows_ref, *refs):
    sources, out_ref, ups, downs, sems = refs[:8], refs[8], refs[9], refs[10], refs[11]
    copies = fetch(
        [(sources[j + 4 * kind], held.at[j]) for j in range(4) for kind, held in ((0, ups), (1, downs))],
        sems,
    )
    targets, _, per_target, double = rows_ref.shape
    quarter = double // 2
    count = targets * per_target
    hidden_count = ups.shape[2]
    me = me_ref[0]
    preact = jnp.zeros((count, hidden_count), F32)
    back = jnp.zeros((count, hidden_count), F32)
    for j in range(4):
        both = rows_ref[:, me ^ j].reshape(count, double)
        copies[2 * j].wait()
        preact = preact + jnp.dot(both[:, :quarter], ups[j], preferred_element_type=F32)
        copies[2 * j + 1].wait()
        back = back + lax.dot_general(
            both[:, quarter:], downs[j], (((1,), (1,)), ((), ())), preferred_element_type=F32
        )
    sigmoid = 1.0 / (1.0 + jnp.exp(-preact))
    out_ref[:, :hidden_count] = (preact * sigmoid).astype(BF16)
    out_ref[:, hidden_count:] = (back * sigmoid * (1.0 + preact * (1.0 - sigmoid))).astype(BF16)


def expert_out_kernel(me_ref, acts_ref, *refs):
    sources, out_ref, downs, sems = refs[:4], refs[4], refs[5], refs[6]
    copies = fetch([(sources[j], downs.at[j]) for j in range(4)], sems)
    targets, _, per_target, quarter = out_ref.shape
    hidden = acts_ref[:, : downs.shape[1]]
    me = me_ref[0]
    for j in range(4):
        copies[j].wait()
        part = jnp.dot(hidden, downs[j], preferred_element_type=F32).astype(BF16)
        out_ref[:, me ^ j] = part.reshape(targets, per_target, quarter)


def combine_kernel(share_ref, returned_ref, out_ref):
    targets, quarters, per_target, quarter = returned_ref.shape
    shares = split3(share_ref[...])
    for q in range(quarters):
        rows = returned_ref[:, q].reshape(targets * per_target, quarter)
        mixed = sum(jnp.dot(part, rows, preferred_element_type=F32) for part in shares)
        out_ref[:, q * quarter : (q + 1) * quarter] = mixed.astype(BF16)


def moment_kernel(
    me_ref, rows_ref, a0, a1, a2, a3, up_hbm, down_hbm, out_ref, up_ref, down_ref, sems
):
    copies = fetch([(up_hbm, up_ref), (down_hbm, down_ref)], sems)
    acts = (a0, a1, a2, a3)
    me = me_ref[0]
    features, hidden_count = up_ref.shape
    over_rows = (((0,), (0,)), ((), ()))
    up_grad = jnp.zeros((features, hidden_count), F32)
    down_grad = jnp.zeros((hidden_count, features), F32)
    for j in range(4):
        rows = rows_ref[me ^ j].reshape(acts[j].shape[0], 2 * features)
        up_grad = up_grad + lax.dot_general(
            rows[:, :features],
            acts[j][:, hidden_count:],
            over_rows,
            preferred_element_type=F32,
        )
        down_grad = down_grad + lax.dot_general(
            acts[j][:, :hidden_count],
            rows[:, features:],
            over_rows,
            preferred_element_type=F32,
        )
    rest = 1.0 - MOMENT_DECAY
    for copy in copies:
        copy.wait()
    up = (MOMENT_DECAY * up_ref[...].astype(F32) + rest * up_grad).astype(BF16)
    down = (MOMENT_DECAY * down_ref[...].astype(F32) + rest * down_grad).astype(BF16)
    up = up.reshape(32, 16, hidden_count)
    for j in range(2):
        for c in range(3):
            at = j * 384 + c * 128
            out_ref[j * 32 : (j + 1) * 32, c * 16 : (c + 1) * 16, :] = up[:, :, at : at + 128]
    down = down.reshape(16, 48, features)
    for j in range(4):
        out_ref[64 + j * 16 : 80 + j * 16] = down[:, :, j * 128 : (j + 1) * 128]


def pick_kernel(partner_ref, spread_ref, out_ref):
    def step(slot, carry):
        out_ref[slot] = spread_ref[partner_ref[slot]]
        return carry

    lax.fori_loop(0, out_ref.shape[0], step, 0, unroll=8)


def unpack_kernel(pieces_ref, up_ref, down_ref):
    for j in range(2):
        for c in range(3):
            at = j * 384 + c * 128
            part = pieces_ref[j * 32 : (j + 1) * 32, c * 16 : (c + 1) * 16, :]
            up_ref[:, at : at + 128] = part.reshape(512, 128)
    for j in range(4):
        part = pieces_ref[64 + j * 16 : 80 + j * 16]
        down_ref[:, j * 128 : (j + 1) * 128] = part.reshape(768, 128)


def shape_of(dims, dtype=BF16):
    return jax.ShapeDtypeStruct(dims, dtype)


def body(
    tokens,
    expert_ids,
    route_weight,
    cotangent,
    holder,
    partner,
    up_weight,
    down_weight,
    up_moment,
    down_moment,
):
    plane = lax.axis_index("zh").reshape(1).astype(jnp.int32)
    me = lax.axis_index(DP_AXES).reshape(1).astype(jnp.int32)

    packed = call(pack_kernel, "pack", shape_of((24, 4224)), [VMEM] * 5, 10**6, 4 * 10**5)(
        tokens, cotangent, expert_ids.T, route_weight.T, holder.reshape(1, -1)
    )
    gathered = lax.all_gather(packed, "zh", axis=0, tiled=True)

    up0, down0 = up_weight[0], down_weight[0]
    up2, down2 = lax.ppermute(up0, "yl", FLIP), lax.ppermute(down0, "yl", FLIP)
    up1, down1 = lax.ppermute(up0, "core", FLIP), lax.ppermute(down0, "core", FLIP)
    up3, down3 = lax.ppermute(up2, "core", FLIP), lax.ppermute(down2, "core", FLIP)
    gathered, up1, up2, up3, down1, down2, down3 = lax.optimization_barrier(
        (gathered, up1, up2, up3, down1, down2, down3)
    )
    ups, downs = (up0, up1, up2, up3), (down0, down1, down2, down3)

    outgoing, share = call(
        select_kernel,
        "select",
        (shape_of((16, 4, 16, 1024)), shape_of((192, 256), F32)),
        [SMEM, VMEM],
        10**9,
        4 * 10**6,
    )(plane, gathered)
    rows = lax.all_to_all(outgoing, GROUP_AXES, split_axis=0, concat_axis=0, tiled=True)
    by_feature = lax.all_to_all(
        rows.transpose(1, 0, 2, 3), DP_AXES, split_axis=0, concat_axis=0, tiled=True
    )

    acts = call(
        forward_kernel,
        "forward",
        shape_of((256, 1536)),
        [SMEM, VMEM] + [HBM] * 8,
        16 * 10**8,
        9 * 10**6,
        (
            pltpu.VMEM((4, 512, 768), BF16),
            pltpu.VMEM((4, 768, 512), BF16),
            pltpu.SemaphoreType.DMA((8,)),
        ),
    )(me, rows, *ups, *downs)
    acts2 = lax.ppermute(acts, "yl", FLIP)
    acts1 = lax.ppermute(acts, "core", FLIP)

    expert_out = call(
        expert_out_kernel,
        "expert_out",
        shape_of((16, 4, 16, 512)),
        [SMEM, VMEM] + [HBM] * 4,
        8 * 10**8,
        5 * 10**6,
        (pltpu.VMEM((4, 768, 512), BF16), pltpu.SemaphoreType.DMA((4,))),
    )(me, acts, *downs)

    by_feature, acts1, acts2, expert_out = lax.optimization_barrier(
        (by_feature, acts1, acts2, expert_out)
    )
    acts3 = lax.ppermute(acts2, "core", FLIP)
    returned = lax.all_to_all(expert_out, GROUP_AXES, split_axis=0, concat_axis=0, tiled=True)
    partial = call(
        combine_kernel, "combine", shape_of((192, 2048)), [VMEM, VMEM], 6 * 10**8, 2 * 10**6, (), 12
    )(share, returned)
    pieces = call(
        moment_kernel,
        "moments",
        shape_of((128, 48, 128)),
        [SMEM] + [VMEM] * 5 + [HBM] * 2,
        32 * 10**8,
        9 * 10**6,
        (
            pltpu.VMEM((512, 768), BF16),
            pltpu.VMEM((768, 512), BF16),
            pltpu.SemaphoreType.DMA((2,)),
        ),
    )(me, by_feature, acts, acts1, acts2, acts3, up_moment[0], down_moment[0])

    layer_out = lax.psum_scatter(partial, "zh", scatter_dimension=0, tiled=True)

    spread = lax.all_to_all(pieces, SLOT_AXES, split_axis=0, concat_axis=0, tiled=True)
    spread, layer_out = lax.optimization_barrier((spread, layer_out))
    chosen = call(
        pick_kernel, "pick", shape_of((128, 48, 128)), [SMEM, VMEM], 0, 3 * 10**6, (), 12
    )(partner, spread)
    landed = lax.all_to_all(chosen, SLOT_AXES, split_axis=0, concat_axis=0, tiled=True)
    new_up, new_down = call(
        unpack_kernel,
        "unpack",
        (shape_of((512, 768)), shape_of((768, 512))),
        [VMEM],
        0,
        3 * 10**6,
        (),
        12,
    )(landed)
    return layer_out, new_up[None], new_down[None]


def solution(mesh):
    wide = Mesh(mesh.devices.reshape(2, 8, 2, 4, 2, 2), AXES)
    return jax.shard_map(
        body,
        mesh=wide,
        in_specs=(
            P(AXES, None),
            P(AXES, None),
            P(AXES, None),
            P(AXES, None),
            P(),
            P(),
            P(SLOT_AXES, DP_AXES, None),
            P(SLOT_AXES, None, DP_AXES),
            P(SLOT_AXES, DP_AXES, None),
            P(SLOT_AXES, None, DP_AXES),
        ),
        out_specs=(
            P(AXES, None),
            P(SLOT_AXES, DP_AXES, None),
            P(SLOT_AXES, None, DP_AXES),
        ),
        check_vma=False,
    )
```

```python
import jax
import jax.numpy as jnp
from jax import lax
from jax.experimental import pallas as pl
from jax.experimental.pallas import tpu as pltpu
from jax.sharding import Mesh, PartitionSpec as P

MOMENT_DECAY = 0.9
AXES = ("yh", "zh", "zp", "x", "yl", "core")
SLOT_AXES = ("yh", "zh", "zp", "x")
GROUP_AXES = ("yh", "zp", "x")
DP_AXES = ("yl", "core")
BF16 = jnp.bfloat16
F32 = jnp.float32
FLIP = [(0, 1), (1, 0)]
VMEM = pl.BlockSpec(memory_space=pltpu.VMEM)
SMEM = pl.BlockSpec(memory_space=pltpu.SMEM)
HBM = pl.BlockSpec(memory_space=pltpu.HBM)


def call(kernel, name, out_shape, in_specs, flops, moved, scratch=(), grant=62):
    outs = jax.tree.map(lambda _: VMEM, out_shape)
    return pl.pallas_call(
        kernel,
        name=name,
        out_shape=out_shape,
        in_specs=in_specs,
        out_specs=outs,
        scratch_shapes=scratch,
        compiler_params=pltpu.CompilerParams(vmem_limit_bytes=grant * 1024 * 1024),
        cost_estimate=pl.CostEstimate(flops=flops, bytes_accessed=moved, transcendentals=0),
    )


def split3(value):
    high = value.astype(BF16)
    rest = value - high.astype(F32)
    middle = rest.astype(BF16)
    low = (rest - middle.astype(F32)).astype(BF16)
    return high, middle, low


def fetch(pairs, sems):
    copies = [
        pltpu.make_async_copy(source, target, sems.at[i]) for i, (source, target) in enumerate(pairs)
    ]
    for copy in copies:
        copy.start()
    return copies


def pack_kernel(tok_ref, cot_ref, ids_ref, weight_ref, holder_ref, out_ref):
    top, rows = ids_ref.shape
    width = tok_ref.shape[1]
    experts = holder_ref.shape[1]
    row_at = lax.broadcasted_iota(jnp.int32, (rows, rows), 0)
    column_at = lax.broadcasted_iota(jnp.int32, (rows, rows), 1)
    same = (row_at == column_at).astype(BF16)

    def turned(value):
        return lax.dot_general(
            same, value.astype(BF16), (((1,), (1,)), ((), ())), preferred_element_type=F32
        )

    ids = turned(ids_ref[...].astype(F32))
    parts = [turned(part) for part in split3(weight_ref[...])]
    lane = lax.broadcasted_iota(jnp.int32, (rows, experts), 1).astype(F32)
    hits = [(ids[:, k : k + 1] == lane).astype(F32) for k in range(top)]
    hit = sum(hits[1:], hits[0])
    earlier = (row_at > column_at).astype(BF16)
    before = jnp.dot(earlier, hit.astype(BF16), preferred_element_type=F32)
    base = 2.0 * holder_ref[...].astype(F32) + before
    meta_lane = lax.broadcasted_iota(jnp.int32, (rows, 128), 1)
    meta = jnp.zeros((rows, 128), F32)
    for k in range(top):
        code = jnp.sum(hits[k] * base, axis=1, keepdims=True)
        meta = jnp.where(meta_lane == k, code, meta)
        for place, part in enumerate(parts):
            meta = jnp.where(meta_lane == (place + 1) * top + k, part[:, k : k + 1], meta)
    out_ref[:, :width] = tok_ref[...]
    out_ref[:, width : 2 * width] = cot_ref[...]
    out_ref[:, 2 * width :] = meta.astype(BF16)


def select_kernel(plane_ref, gathered_ref, out_ref, share_ref):
    total = gathered_ref.shape[0]
    targets, quarters, per_target, quarter = out_ref.shape
    width = quarters * quarter
    top = 8
    rows = targets * per_target
    block = total // (per_target // 2)
    plane = plane_ref[0]
    meta = gathered_ref[:, 2 * width :].astype(F32)
    row = lax.broadcasted_iota(jnp.int32, (total, rows), 1)
    token = lax.broadcasted_iota(jnp.int32, (total, rows), 0)
    target = row >> 4
    first = ((row >> 1) & 7) * block
    inside = (token >= first) & (token < first + block)
    slot = (target >> 3) * 64 + plane * 8 + (target & 7)
    wanted = jnp.where(inside, slot * 2 + (row & 1), -1).astype(F32)
    picked = jnp.zeros((total, rows), F32)
    share = jnp.zeros((total, rows), F32)
    for k in range(top):
        match = meta[:, k : k + 1] == wanted
        weight = (
            meta[:, top + k : top + k + 1]
            + meta[:, 2 * top + k : 2 * top + k + 1]
            + meta[:, 3 * top + k : 3 * top + k + 1]
        )
        picked = jnp.where(match, 1.0, picked)
        share = jnp.where(match, weight, share)
    share_ref[...] = share
    picked_t = jnp.transpose(picked).astype(BF16)
    for q in range(quarters):
        tok = gathered_ref[:, q * quarter : (q + 1) * quarter]
        sent = jnp.dot(picked_t, tok, preferred_element_type=F32).astype(BF16)
        out_ref[:, q] = sent.reshape(targets, per_target, quarter)


def scale_kernel(share_ref, gathered_ref, out_ref):
    targets, quarters, per_target, quarter = out_ref.shape
    width = quarters * quarter
    shares_t = split3(jnp.transpose(share_ref[...]))
    for q in range(quarters):
        cot = gathered_ref[:, width + q * quarter : width + (q + 1) * quarter]
        grads = sum(jnp.dot(part, cot, preferred_element_type=F32) for part in shares_t)
        out_ref[:, q] = grads.astype(BF16).reshape(targets, per_target, quarter)


def hidden_kernel(me_ref, rows_ref, *refs):
    sources, hidden_ref, slope_ref, ups, sems = refs[:4], refs[4], refs[5], refs[6], refs[7]
    copies = fetch([(sources[j], ups.at[j]) for j in range(4)], sems)
    targets, _, per_target, quarter = rows_ref.shape
    count = targets * per_target
    me = me_ref[0]
    preact = jnp.zeros((count, ups.shape[2]), F32)
    for j in range(4):
        part = rows_ref[:, me ^ j].reshape(count, quarter)
        copies[j].wait()
        preact = preact + jnp.dot(part, ups[j], preferred_element_type=F32)
    sigmoid = 1.0 / (1.0 + jnp.exp(-preact))
    hidden_ref[...] = (preact * sigmoid).astype(BF16)
    slope_ref[...] = sigmoid * (1.0 + preact * (1.0 - sigmoid))


def back_kernel(me_ref, rows_ref, slope_ref, *refs):
    sources, out_ref, downs, sems = refs[:4], refs[4], refs[5], refs[6]
    copies = fetch([(sources[j], downs.at[j]) for j in range(4)], sems)
    targets, _, per_target, quarter = rows_ref.shape
    count = targets * per_target
    me = me_ref[0]
    back = jnp.zeros(slope_ref.shape, F32)
    for j in range(4):
        part = rows_ref[:, me ^ j].reshape(count, quarter)
        copies[j].wait()
        back = back + lax.dot_general(
            part, downs[j], (((1,), (1,)), ((), ())), preferred_element_type=F32
        )
    out_ref[...] = (back * slope_ref[...]).astype(BF16)


def expert_out_kernel(me_ref, hidden_ref, *refs):
    sources, out_ref, downs, sems = refs[:4], refs[4], refs[5], refs[6]
    copies = fetch([(sources[j], downs.at[j]) for j in range(4)], sems)
    targets, _, per_target, quarter = out_ref.shape
    hidden = hidden_ref[...]
    me = me_ref[0]
    for j in range(4):
        copies[j].wait()
        part = jnp.dot(hidden, downs[j], preferred_element_type=F32).astype(BF16)
        out_ref[:, me ^ j] = part.reshape(targets, per_target, quarter)


def combine_kernel(share_ref, returned_ref, out_ref):
    targets, quarters, per_target, quarter = returned_ref.shape
    shares = split3(share_ref[...])
    for q in range(quarters):
        rows = returned_ref[:, q].reshape(targets * per_target, quarter)
        mixed = sum(jnp.dot(part, rows, preferred_element_type=F32) for part in shares)
        out_ref[:, q * quarter : (q + 1) * quarter] = mixed.astype(BF16)


def moment_kernel(
    me_ref, rows_ref, h0, h1, h2, h3, g0, g1, g2, g3, up_hbm, down_hbm, out_ref, up_ref, down_ref, sems
):
    copies = fetch([(up_hbm, up_ref), (down_hbm, down_ref)], sems)
    hiddens, pre_grads = (h0, h1, h2, h3), (g0, g1, g2, g3)
    me = me_ref[0]
    features, hidden_count = up_ref.shape
    over_rows = (((0,), (0,)), ((), ()))
    up_grad = jnp.zeros((features, hidden_count), F32)
    down_grad = jnp.zeros((hidden_count, features), F32)
    for j in range(4):
        rows = rows_ref[me ^ j].reshape(hiddens[j].shape[0], 2 * features)
        up_grad = up_grad + lax.dot_general(
            rows[:, :features],
            pre_grads[j][...],
            over_rows,
            preferred_element_type=F32,
        )
        down_grad = down_grad + lax.dot_general(
            hiddens[j][...],
            rows[:, features:],
            over_rows,
            preferred_element_type=F32,
        )
    rest = 1.0 - MOMENT_DECAY
    for copy in copies:
        copy.wait()
    up = (MOMENT_DECAY * up_ref[...].astype(F32) + rest * up_grad).astype(BF16)
    down = (MOMENT_DECAY * down_ref[...].astype(F32) + rest * down_grad).astype(BF16)
    up = up.reshape(32, 16, hidden_count)
    for j in range(2):
        for c in range(3):
            at = j * 384 + c * 128
            out_ref[j * 32 : (j + 1) * 32, c * 16 : (c + 1) * 16, :] = up[:, :, at : at + 128]
    down = down.reshape(16, 48, features)
    for j in range(4):
        out_ref[64 + j * 16 : 80 + j * 16] = down[:, :, j * 128 : (j + 1) * 128]


def pick_kernel(partner_ref, spread_ref, out_ref):
    def step(slot, carry):
        out_ref[slot] = spread_ref[partner_ref[slot]]
        return carry

    lax.fori_loop(0, out_ref.shape[0], step, 0, unroll=8)


def unpack_kernel(pieces_ref, up_ref, down_ref):
    for j in range(2):
        for c in range(3):
            at = j * 384 + c * 128
            part = pieces_ref[j * 32 : (j + 1) * 32, c * 16 : (c + 1) * 16, :]
            up_ref[:, at : at + 128] = part.reshape(512, 128)
    for j in range(4):
        part = pieces_ref[64 + j * 16 : 80 + j * 16]
        down_ref[:, j * 128 : (j + 1) * 128] = part.reshape(768, 128)


def shape_of(dims, dtype=BF16):
    return jax.ShapeDtypeStruct(dims, dtype)


def body(
    tokens,
    expert_ids,
    route_weight,
    cotangent,
    holder,
    partner,
    up_weight,
    down_weight,
    up_moment,
    down_moment,
):
    plane = lax.axis_index("zh").reshape(1).astype(jnp.int32)
    me = lax.axis_index(DP_AXES).reshape(1).astype(jnp.int32)

    packed = call(pack_kernel, "pack", shape_of((24, 4224)), [VMEM] * 5, 10**6, 4 * 10**5)(
        tokens, cotangent, expert_ids.T, route_weight.T, holder.reshape(1, -1)
    )
    gathered = lax.all_gather(packed, "zh", axis=0, tiled=True)

    up0, down0 = up_weight[0], down_weight[0]
    up2, down2 = lax.ppermute(up0, "yl", FLIP), lax.ppermute(down0, "yl", FLIP)
    up1, down1 = lax.ppermute(up0, "core", FLIP), lax.ppermute(down0, "core", FLIP)
    up3, down3 = lax.ppermute(up2, "core", FLIP), lax.ppermute(down2, "core", FLIP)
    gathered, up1, up2, up3, down1, down2, down3 = lax.optimization_barrier(
        (gathered, up1, up2, up3, down1, down2, down3)
    )
    ups, downs = (up0, up1, up2, up3), (down0, down1, down2, down3)

    tokens_out, share = call(
        select_kernel,
        "select",
        (shape_of((16, 4, 16, 512)), shape_of((192, 256), F32)),
        [SMEM, VMEM],
        3 * 10**8,
        3 * 10**6,
    )(plane, gathered)
    grads_out = call(
        scale_kernel, "scale", shape_of((16, 4, 16, 512)), [VMEM, VMEM], 7 * 10**8, 3 * 10**6
    )(share, gathered)
    token_rows = lax.all_to_all(tokens_out, GROUP_AXES, split_axis=0, concat_axis=0, tiled=True)
    grads_out, token_rows = lax.optimization_barrier((grads_out, token_rows))
    grad_rows = lax.all_to_all(grads_out, GROUP_AXES, split_axis=0, concat_axis=0, tiled=True)

    down_scratch = (pltpu.VMEM((4, 768, 512), BF16), pltpu.SemaphoreType.DMA((4,)))
    hidden, slope = call(
        hidden_kernel,
        "hidden",
        (shape_of((256, 768)), shape_of((256, 768), F32)),
        [SMEM, VMEM] + [HBM] * 4,
        8 * 10**8,
        5 * 10**6,
        (pltpu.VMEM((4, 512, 768), BF16), pltpu.SemaphoreType.DMA((4,))),
    )(me, token_rows, *ups)
    hidden2 = lax.ppermute(hidden, "yl", FLIP)
    hidden1 = lax.ppermute(hidden, "core", FLIP)
    expert_out = call(
        expert_out_kernel,
        "expert_out",
        shape_of((16, 4, 16, 512)),
        [SMEM, VMEM] + [HBM] * 4,
        8 * 10**8,
        5 * 10**6,
        down_scratch,
    )(me, hidden, *downs)

    grad_rows, hidden1, hidden2, expert_out = lax.optimization_barrier(
        (grad_rows, hidden1, hidden2, expert_out)
    )
    returned = lax.all_to_all(expert_out, GROUP_AXES, split_axis=0, concat_axis=0, tiled=True)
    pre_grad = call(
        back_kernel,
        "back",
        shape_of((256, 768)),
        [SMEM, VMEM, VMEM] + [HBM] * 4,
        8 * 10**8,
        5 * 10**6,
        down_scratch,
    )(me, grad_rows, slope, *downs)
    pre_grad2 = lax.ppermute(pre_grad, "yl", FLIP)
    pre_grad1 = lax.ppermute(pre_grad, "core", FLIP)
    both = jnp.concatenate([token_rows, grad_rows], axis=-1).transpose(1, 0, 2, 3)

    both, returned, pre_grad1, pre_grad2 = lax.optimization_barrier(
        (both, returned, pre_grad1, pre_grad2)
    )
    by_feature = lax.all_to_all(both, DP_AXES, split_axis=0, concat_axis=0, tiled=True)
    hidden3 = lax.ppermute(hidden2, "core", FLIP)
    pre_grad3 = lax.ppermute(pre_grad2, "core", FLIP)
    partial = call(
        combine_kernel, "combine", shape_of((192, 2048)), [VMEM, VMEM], 6 * 10**8, 2 * 10**6, (), 12
    )(share, returned)
    by_feature, _ = lax.optimization_barrier((by_feature, partial))
    layer_out = lax.psum_scatter(partial, "zh", scatter_dimension=0, tiled=True)

    pieces = call(
        moment_kernel,
        "moments",
        shape_of((128, 48, 128)),
        [SMEM] + [VMEM] * 9 + [HBM] * 2,
        32 * 10**8,
        9 * 10**6,
        (
            pltpu.VMEM((512, 768), BF16),
            pltpu.VMEM((768, 512), BF16),
            pltpu.SemaphoreType.DMA((2,)),
        ),
    )(
        me,
        by_feature,
        hidden,
        hidden1,
        hidden2,
        hidden3,
        pre_grad,
        pre_grad1,
        pre_grad2,
        pre_grad3,
        up_moment[0],
        down_moment[0],
    )
    pieces, layer_out = lax.optimization_barrier((pieces, layer_out))
    spread = lax.all_to_all(pieces, SLOT_AXES, split_axis=0, concat_axis=0, tiled=True)
    chosen = call(
        pick_kernel, "pick", shape_of((128, 48, 128)), [SMEM, VMEM], 0, 3 * 10**6, (), 12
    )(partner, spread)
    landed = lax.all_to_all(chosen, SLOT_AXES, split_axis=0, concat_axis=0, tiled=True)
    new_up, new_down = call(
        unpack_kernel,
        "unpack",
        (shape_of((512, 768)), shape_of((768, 512))),
        [VMEM],
        0,
        3 * 10**6,
        (),
        12,
    )(landed)
    return layer_out, new_up[None], new_down[None]


def solution(mesh):
    wide = Mesh(mesh.devices.reshape(2, 8, 2, 4, 2, 2), AXES)
    return jax.shard_map(
        body,
        mesh=wide,
        in_specs=(
            P(AXES, None),
            P(AXES, None),
            P(AXES, None),
            P(AXES, None),
            P(),
            P(),
            P(SLOT_AXES, DP_AXES, None),
            P(SLOT_AXES, None, DP_AXES),
            P(SLOT_AXES, DP_AXES, None),
            P(SLOT_AXES, None, DP_AXES),
        ),
        out_specs=(
            P(AXES, None),
            P(SLOT_AXES, DP_AXES, None),
            P(SLOT_AXES, None, DP_AXES),
        ),
        check_vma=False,
    )
```

```python
import jax
import jax.numpy as jnp
from jax import lax
from jax.experimental import pallas as pl
from jax.experimental.pallas import tpu as pltpu
from jax.sharding import Mesh, PartitionSpec as P

MOMENT_DECAY = 0.9
AXES = ("yh", "zh", "zp", "x", "yl", "core")
SLOT_AXES = ("yh", "zh", "zp", "x")
GROUP_AXES = ("yh", "zp", "x")
DP_AXES = ("yl", "core")
BF16 = jnp.bfloat16
F32 = jnp.float32
FLIP = [(0, 1), (1, 0)]
VMEM = pl.BlockSpec(memory_space=pltpu.VMEM)
SMEM = pl.BlockSpec(memory_space=pltpu.SMEM)
HBM = pl.BlockSpec(memory_space=pltpu.HBM)


def call(kernel, name, out_shape, in_specs, flops, moved, scratch=(), grant=62):
    outs = jax.tree.map(lambda _: VMEM, out_shape)
    return pl.pallas_call(
        kernel,
        name=name,
        out_shape=out_shape,
        in_specs=in_specs,
        out_specs=outs,
        scratch_shapes=scratch,
        compiler_params=pltpu.CompilerParams(vmem_limit_bytes=grant * 1024 * 1024),
        cost_estimate=pl.CostEstimate(flops=flops, bytes_accessed=moved, transcendentals=0),
    )


def split3(value):
    high = value.astype(BF16)
    rest = value - high.astype(F32)
    middle = rest.astype(BF16)
    low = (rest - middle.astype(F32)).astype(BF16)
    return high, middle, low


def fetch(pairs, sems):
    copies = [
        pltpu.make_async_copy(source, target, sems.at[i]) for i, (source, target) in enumerate(pairs)
    ]
    for copy in copies:
        copy.start()
    return copies


def pack_kernel(tok_ref, ids_ref, weight_ref, holder_ref, out_ref):
    top, rows = ids_ref.shape
    width = tok_ref.shape[1]
    experts = holder_ref.shape[1]
    row_at = lax.broadcasted_iota(jnp.int32, (rows, rows), 0)
    column_at = lax.broadcasted_iota(jnp.int32, (rows, rows), 1)
    same = (row_at == column_at).astype(BF16)

    def turned(value):
        return lax.dot_general(
            same, value.astype(BF16), (((1,), (1,)), ((), ())), preferred_element_type=F32
        )

    ids = turned(ids_ref[...].astype(F32))
    parts = [turned(part) for part in split3(weight_ref[...])]
    lane = lax.broadcasted_iota(jnp.int32, (rows, experts), 1).astype(F32)
    hits = [(ids[:, k : k + 1] == lane).astype(F32) for k in range(top)]
    hit = sum(hits[1:], hits[0])
    earlier = (row_at > column_at).astype(BF16)
    before = jnp.dot(earlier, hit.astype(BF16), preferred_element_type=F32)
    base = 2.0 * holder_ref[...].astype(F32) + before
    meta_lane = lax.broadcasted_iota(jnp.int32, (rows, 128), 1)
    meta = jnp.zeros((rows, 128), F32)
    for k in range(top):
        code = jnp.sum(hits[k] * base, axis=1, keepdims=True)
        meta = jnp.where(meta_lane == k, code, meta)
        for place, part in enumerate(parts):
            meta = jnp.where(meta_lane == (place + 1) * top + k, part[:, k : k + 1], meta)
    out_ref[:, :width] = tok_ref[...]
    out_ref[:, width:] = meta.astype(BF16)


def select_kernel(plane_ref, gathered_ref, cots_ref, out_ref, share_ref):
    total = gathered_ref.shape[0]
    targets, quarters, per_target, _ = out_ref.shape
    quarter = out_ref.shape[3] // 2
    width = quarters * quarter
    top = 8
    rows = targets * per_target
    block = total // (per_target // 2)
    plane = plane_ref[0]
    meta = gathered_ref[:, width:].astype(F32)
    row = lax.broadcasted_iota(jnp.int32, (total, rows), 1)
    token = lax.broadcasted_iota(jnp.int32, (total, rows), 0)
    target = row >> 4
    first = ((row >> 1) & 7) * block
    inside = (token >= first) & (token < first + block)
    slot = (target >> 3) * 64 + plane * 8 + (target & 7)
    wanted = jnp.where(inside, slot * 2 + (row & 1), -1).astype(F32)
    picked = jnp.zeros((total, rows), F32)
    share = jnp.zeros((total, rows), F32)
    for k in range(top):
        match = meta[:, k : k + 1] == wanted
        weight = (
            meta[:, top + k : top + k + 1]
            + meta[:, 2 * top + k : 2 * top + k + 1]
            + meta[:, 3 * top + k : 3 * top + k + 1]
        )
        picked = jnp.where(match, 1.0, picked)
        share = jnp.where(match, weight, share)
    share_ref[...] = share
    picked_t = jnp.transpose(picked).astype(BF16)
    shares_t = split3(jnp.transpose(share))
    for q in range(quarters):
        at = q * quarter
        sent = jnp.dot(
            picked_t, gathered_ref[:, at : at + quarter], preferred_element_type=F32
        ).astype(BF16)
        out_ref[:, q, :, :quarter] = sent.reshape(targets, per_target, quarter)
        cot = cots_ref[:, at : at + quarter]
        grads = sum(jnp.dot(part, cot, preferred_element_type=F32) for part in shares_t)
        out_ref[:, q, :, quarter:] = grads.astype(BF16).reshape(targets, per_target, quarter)


def forward_kernel(me_ref, rows_ref, *refs):
    sources, out_ref, ups, downs, sems = refs[:8], refs[8], refs[9], refs[10], refs[11]
    copies = fetch(
        [(sources[j + 4 * kind], held.at[j]) for j in range(4) for kind, held in ((0, ups), (1, downs))],
        sems,
    )
    targets, _, per_target, double = rows_ref.shape
    quarter = double // 2
    count = targets * per_target
    hidden_count = ups.shape[2]
    me = me_ref[0]
    preact = jnp.zeros((count, hidden_count), F32)
    back = jnp.zeros((count, hidden_count), F32)
    for j in range(4):
        both = rows_ref[:, me ^ j].reshape(count, double)
        copies[2 * j].wait()
        preact = preact + jnp.dot(both[:, :quarter], ups[j], preferred_element_type=F32)
        copies[2 * j + 1].wait()
        back = back + lax.dot_general(
            both[:, quarter:], downs[j], (((1,), (1,)), ((), ())), preferred_element_type=F32
        )
    sigmoid = 1.0 / (1.0 + jnp.exp(-preact))
    out_ref[:, :hidden_count] = (preact * sigmoid).astype(BF16)
    out_ref[:, hidden_count:] = (back * sigmoid * (1.0 + preact * (1.0 - sigmoid))).astype(BF16)


def expert_out_kernel(me_ref, acts_ref, *refs):
    sources, out_ref, downs, sems = refs[:4], refs[4], refs[5], refs[6]
    copies = fetch([(sources[j], downs.at[j]) for j in range(4)], sems)
    targets, _, per_target, quarter = out_ref.shape
    hidden = acts_ref[:, : downs.shape[1]]
    me = me_ref[0]
    for j in range(4):
        copies[j].wait()
        part = jnp.dot(hidden, downs[j], preferred_element_type=F32).astype(BF16)
        out_ref[:, me ^ j] = part.reshape(targets, per_target, quarter)


def combine_kernel(share_ref, returned_ref, out_ref):
    targets, quarters, per_target, quarter = returned_ref.shape
    shares = split3(share_ref[...])
    for q in range(quarters):
        rows = returned_ref[:, q].reshape(targets * per_target, quarter)
        mixed = sum(jnp.dot(part, rows, preferred_element_type=F32) for part in shares)
        out_ref[:, q * quarter : (q + 1) * quarter] = mixed.astype(BF16)


def moment_kernel(
    me_ref, rows_ref, a0, a1, a2, a3, up_hbm, down_hbm, out_ref, up_ref, down_ref, sems
):
    copies = fetch([(up_hbm, up_ref), (down_hbm, down_ref)], sems)
    acts = (a0, a1, a2, a3)
    me = me_ref[0]
    features, hidden_count = up_ref.shape
    over_rows = (((0,), (0,)), ((), ()))
    up_grad = jnp.zeros((features, hidden_count), F32)
    down_grad = jnp.zeros((hidden_count, features), F32)
    for j in range(4):
        rows = rows_ref[me ^ j].reshape(acts[j].shape[0], 2 * features)
        up_grad = up_grad + lax.dot_general(
            rows[:, :features],
            acts[j][:, hidden_count:],
            over_rows,
            preferred_element_type=F32,
        )
        down_grad = down_grad + lax.dot_general(
            acts[j][:, :hidden_count],
            rows[:, features:],
            over_rows,
            preferred_element_type=F32,
        )
    rest = 1.0 - MOMENT_DECAY
    for copy in copies:
        copy.wait()
    up = (MOMENT_DECAY * up_ref[...].astype(F32) + rest * up_grad).astype(BF16)
    down = (MOMENT_DECAY * down_ref[...].astype(F32) + rest * down_grad).astype(BF16)
    up = up.reshape(32, 16, hidden_count)
    for j in range(2):
        for c in range(3):
            at = j * 384 + c * 128
            out_ref[j * 32 : (j + 1) * 32, c * 16 : (c + 1) * 16, :] = up[:, :, at : at + 128]
    down = down.reshape(16, 48, features)
    for j in range(4):
        out_ref[64 + j * 16 : 80 + j * 16] = down[:, :, j * 128 : (j + 1) * 128]


def pick_kernel(partner_ref, spread_ref, out_ref):
    def step(slot, carry):
        out_ref[slot] = spread_ref[partner_ref[slot]]
        return carry

    lax.fori_loop(0, out_ref.shape[0], step, 0, unroll=8)


def unpack_kernel(pieces_ref, up_ref, down_ref):
    for j in range(2):
        for c in range(3):
            at = j * 384 + c * 128
            part = pieces_ref[j * 32 : (j + 1) * 32, c * 16 : (c + 1) * 16, :]
            up_ref[:, at : at + 128] = part.reshape(512, 128)
    for j in range(4):
        part = pieces_ref[64 + j * 16 : 80 + j * 16]
        down_ref[:, j * 128 : (j + 1) * 128] = part.reshape(768, 128)


def shape_of(dims, dtype=BF16):
    return jax.ShapeDtypeStruct(dims, dtype)


def body(
    tokens,
    expert_ids,
    route_weight,
    cotangent,
    holder,
    partner,
    up_weight,
    down_weight,
    up_moment,
    down_moment,
):
    plane = lax.axis_index("zh").reshape(1).astype(jnp.int32)
    me = lax.axis_index(DP_AXES).reshape(1).astype(jnp.int32)

    packed = call(pack_kernel, "pack", shape_of((24, 2176)), [VMEM] * 4, 10**6, 2 * 10**5)(
        tokens, expert_ids.T, route_weight.T, holder.reshape(1, -1)
    )
    copies = jnp.broadcast_to(cotangent[None], (8,) + cotangent.shape)
    packed, copies, up0, down0 = lax.optimization_barrier(
        (packed, copies, up_weight[0], down_weight[0])
    )
    gathered = lax.all_gather(packed, "zh", axis=0, tiled=True)
    cots = lax.all_to_all(copies, "zh", split_axis=0, concat_axis=0, tiled=True).reshape(192, 2048)

    up2, down2 = lax.ppermute(up0, "yl", FLIP), lax.ppermute(down0, "yl", FLIP)
    up1, down1 = lax.ppermute(up0, "core", FLIP), lax.ppermute(down0, "core", FLIP)
    up3, down3 = lax.ppermute(up2, "core", FLIP), lax.ppermute(down2, "core", FLIP)
    gathered, cots, up1, up2, up3, down1, down2, down3 = lax.optimization_barrier(
        (gathered, cots, up1, up2, up3, down1, down2, down3)
    )
    ups, downs = (up0, up1, up2, up3), (down0, down1, down2, down3)

    outgoing, share = call(
        select_kernel,
        "select",
        (shape_of((16, 4, 16, 1024)), shape_of((192, 256), F32)),
        [SMEM, VMEM, VMEM],
        10**9,
        4 * 10**6,
    )(plane, gathered, cots)
    rows = lax.all_to_all(outgoing, GROUP_AXES, split_axis=0, concat_axis=0, tiled=True)
    by_feature = lax.all_to_all(
        rows.transpose(1, 0, 2, 3), DP_AXES, split_axis=0, concat_axis=0, tiled=True
    )

    acts = call(
        forward_kernel,
        "forward",
        shape_of((256, 1536)),
        [SMEM, VMEM] + [HBM] * 8,
        16 * 10**8,
        9 * 10**6,
        (
            pltpu.VMEM((4, 512, 768), BF16),
            pltpu.VMEM((4, 768, 512), BF16),
            pltpu.SemaphoreType.DMA((8,)),
        ),
    )(me, rows, *ups, *downs)
    acts2 = lax.ppermute(acts, "yl", FLIP)
    acts1 = lax.ppermute(acts, "core", FLIP)

    expert_out = call(
        expert_out_kernel,
        "expert_out",
        shape_of((16, 4, 16, 512)),
        [SMEM, VMEM] + [HBM] * 4,
        8 * 10**8,
        5 * 10**6,
        (pltpu.VMEM((4, 768, 512), BF16), pltpu.SemaphoreType.DMA((4,))),
    )(me, acts, *downs)

    by_feature, acts1, acts2, expert_out = lax.optimization_barrier(
        (by_feature, acts1, acts2, expert_out)
    )
    acts3 = lax.ppermute(acts2, "core", FLIP)
    returned = lax.all_to_all(expert_out, GROUP_AXES, split_axis=0, concat_axis=0, tiled=True)
    partial = call(
        combine_kernel, "combine", shape_of((192, 2048)), [VMEM, VMEM], 6 * 10**8, 2 * 10**6, (), 12
    )(share, returned)
    pieces = call(
        moment_kernel,
        "moments",
        shape_of((128, 48, 128)),
        [SMEM] + [VMEM] * 5 + [HBM] * 2,
        32 * 10**8,
        9 * 10**6,
        (
            pltpu.VMEM((512, 768), BF16),
            pltpu.VMEM((768, 512), BF16),
            pltpu.SemaphoreType.DMA((2,)),
        ),
    )(me, by_feature, acts, acts1, acts2, acts3, up_moment[0], down_moment[0])

    layer_out = lax.psum_scatter(partial, "zh", scatter_dimension=0, tiled=True)

    spread = lax.all_to_all(pieces, SLOT_AXES, split_axis=0, concat_axis=0, tiled=True)
    spread, layer_out = lax.optimization_barrier((spread, layer_out))
    chosen = call(
        pick_kernel, "pick", shape_of((128, 48, 128)), [SMEM, VMEM], 0, 3 * 10**6, (), 12
    )(partner, spread)
    landed = lax.all_to_all(chosen, SLOT_AXES, split_axis=0, concat_axis=0, tiled=True)
    new_up, new_down = call(
        unpack_kernel,
        "unpack",
        (shape_of((512, 768)), shape_of((768, 512))),
        [VMEM],
        0,
        3 * 10**6,
        (),
        12,
    )(landed)
    return layer_out, new_up[None], new_down[None]


def solution(mesh):
    wide = Mesh(mesh.devices.reshape(2, 8, 2, 4, 2, 2), AXES)
    return jax.shard_map(
        body,
        mesh=wide,
        in_specs=(
            P(AXES, None),
            P(AXES, None),
            P(AXES, None),
            P(AXES, None),
            P(),
            P(),
            P(SLOT_AXES, DP_AXES, None),
            P(SLOT_AXES, None, DP_AXES),
            P(SLOT_AXES, DP_AXES, None),
            P(SLOT_AXES, None, DP_AXES),
        ),
        out_specs=(
            P(AXES, None),
            P(SLOT_AXES, DP_AXES, None),
            P(SLOT_AXES, None, DP_AXES),
        ),
        check_vma=False,
    )
```

```python
import jax
import jax.numpy as jnp
from jax import lax
from jax.experimental import pallas as pl
from jax.experimental.pallas import tpu as pltpu
from jax.sharding import Mesh, PartitionSpec as P

MOMENT_DECAY = 0.9
AXES = ("yh", "zh", "zp", "x", "yl", "core")
SLOT_AXES = ("yh", "zh", "zp", "x")
GROUP_AXES = ("yh", "zp", "x")
DP_AXES = ("yl", "core")
BF16 = jnp.bfloat16
F32 = jnp.float32
FLIP = [(0, 1), (1, 0)]
VMEM = pl.BlockSpec(memory_space=pltpu.VMEM)
SMEM = pl.BlockSpec(memory_space=pltpu.SMEM)
HBM = pl.BlockSpec(memory_space=pltpu.HBM)


def call(kernel, name, out_shape, in_specs, flops, moved, scratch=(), grant=62):
    outs = jax.tree.map(lambda _: VMEM, out_shape)
    return pl.pallas_call(
        kernel,
        name=name,
        out_shape=out_shape,
        in_specs=in_specs,
        out_specs=outs,
        scratch_shapes=scratch,
        compiler_params=pltpu.CompilerParams(vmem_limit_bytes=grant * 1024 * 1024),
        cost_estimate=pl.CostEstimate(flops=flops, bytes_accessed=moved, transcendentals=0),
    )


def split3(value):
    high = value.astype(BF16)
    rest = value - high.astype(F32)
    middle = rest.astype(BF16)
    low = (rest - middle.astype(F32)).astype(BF16)
    return high, middle, low


def fetch(pairs, sems):
    copies = [
        pltpu.make_async_copy(source, target, sems.at[i]) for i, (source, target) in enumerate(pairs)
    ]
    for copy in copies:
        copy.start()
    return copies


def pack_kernel(tok_ref, cot_ref, ids_ref, weight_ref, holder_ref, out_ref):
    top, rows = ids_ref.shape
    width = tok_ref.shape[1]
    experts = holder_ref.shape[1]
    row_at = lax.broadcasted_iota(jnp.int32, (rows, rows), 0)
    column_at = lax.broadcasted_iota(jnp.int32, (rows, rows), 1)
    same = (row_at == column_at).astype(BF16)

    def turned(value):
        return lax.dot_general(
            same, value.astype(BF16), (((1,), (1,)), ((), ())), preferred_element_type=F32
        )

    ids = turned(ids_ref[...].astype(F32))
    parts = [turned(part) for part in split3(weight_ref[...])]
    lane = lax.broadcasted_iota(jnp.int32, (rows, experts), 1).astype(F32)
    hits = [(ids[:, k : k + 1] == lane).astype(F32) for k in range(top)]
    hit = sum(hits[1:], hits[0])
    earlier = (row_at > column_at).astype(BF16)
    before = jnp.dot(earlier, hit.astype(BF16), preferred_element_type=F32)
    base = 2.0 * holder_ref[...].astype(F32) + before
    meta_lane = lax.broadcasted_iota(jnp.int32, (rows, 128), 1)
    meta = jnp.zeros((rows, 128), F32)
    for k in range(top):
        code = jnp.sum(hits[k] * base, axis=1, keepdims=True)
        meta = jnp.where(meta_lane == k, code, meta)
        for place, part in enumerate(parts):
            meta = jnp.where(meta_lane == (place + 1) * top + k, part[:, k : k + 1], meta)
    out_ref[:, :width] = tok_ref[...]
    out_ref[:, width : 2 * width] = cot_ref[...]
    out_ref[:, 2 * width :] = meta.astype(BF16)


def select_kernel(plane_ref, gathered_ref, out_ref, share_ref):
    total = gathered_ref.shape[0]
    targets, quarters, per_target, _ = out_ref.shape
    quarter = out_ref.shape[3] // 2
    width = quarters * quarter
    top = 8
    rows = targets * per_target
    block = total // (per_target // 2)
    plane = plane_ref[0]
    meta = gathered_ref[:, 2 * width :].astype(F32)
    row = lax.broadcasted_iota(jnp.int32, (total, rows), 1)
    token = lax.broadcasted_iota(jnp.int32, (total, rows), 0)
    target = row >> 4
    first = ((row >> 1) & 7) * block
    inside = (token >= first) & (token < first + block)
    slot = (target >> 3) * 64 + plane * 8 + (target & 7)
    wanted = jnp.where(inside, slot * 2 + (row & 1), -1).astype(F32)
    picked = jnp.zeros((total, rows), F32)
    share = jnp.zeros((total, rows), F32)
    for k in range(top):
        match = meta[:, k : k + 1] == wanted
        weight = (
            meta[:, top + k : top + k + 1]
            + meta[:, 2 * top + k : 2 * top + k + 1]
            + meta[:, 3 * top + k : 3 * top + k + 1]
        )
        picked = jnp.where(match, 1.0, picked)
        share = jnp.where(match, weight, share)
    share_ref[...] = share
    picked_t = jnp.transpose(picked).astype(BF16)
    shares_t = split3(jnp.transpose(share))
    for q in range(quarters):
        at = q * quarter
        sent = jnp.dot(
            picked_t, gathered_ref[:, at : at + quarter], preferred_element_type=F32
        ).astype(BF16)
        out_ref[:, q, :, :quarter] = sent.reshape(targets, per_target, quarter)
        cot = gathered_ref[:, width + at : width + at + quarter]
        grads = sum(jnp.dot(part, cot, preferred_element_type=F32) for part in shares_t)
        out_ref[:, q, :, quarter:] = grads.astype(BF16).reshape(targets, per_target, quarter)


def forward_kernel(me_ref, rows_ref, *refs):
    sources, hidden_ref, pre_grad_ref, ups, downs, sems = refs[:8], *refs[8:]
    copies = fetch(
        [(sources[j + 4 * kind], held.at[j]) for j in range(4) for kind, held in ((0, ups), (1, downs))],
        sems,
    )
    targets, _, per_target, double = rows_ref.shape
    quarter = double // 2
    count = targets * per_target
    hidden_count = ups.shape[2]
    me = me_ref[0]
    preact = jnp.zeros((count, hidden_count), F32)
    back = jnp.zeros((count, hidden_count), F32)
    for j in range(4):
        both = rows_ref[:, me ^ j].reshape(count, double)
        copies[2 * j].wait()
        preact = preact + jnp.dot(both[:, :quarter], ups[j], preferred_element_type=F32)
        copies[2 * j + 1].wait()
        back = back + lax.dot_general(
            both[:, quarter:], downs[j], (((1,), (1,)), ((), ())), preferred_element_type=F32
        )
    sigmoid = 1.0 / (1.0 + jnp.exp(-preact))
    hidden_ref[...] = (preact * sigmoid).astype(BF16)
    pre_grad_ref[...] = (back * sigmoid * (1.0 + preact * (1.0 - sigmoid))).astype(BF16)


def expert_out_kernel(me_ref, hidden_ref, *refs):
    sources, out_ref, downs, sems = refs[:4], refs[4], refs[5], refs[6]
    copies = fetch([(sources[j], downs.at[j]) for j in range(4)], sems)
    targets, _, per_target, quarter = out_ref.shape
    hidden = hidden_ref[...]
    me = me_ref[0]
    for j in range(4):
        copies[j].wait()
        part = jnp.dot(hidden, downs[j], preferred_element_type=F32).astype(BF16)
        out_ref[:, me ^ j] = part.reshape(targets, per_target, quarter)


def combine_kernel(share_ref, returned_ref, out_ref):
    targets, quarters, per_target, quarter = returned_ref.shape
    shares = split3(share_ref[...])
    for q in range(quarters):
        rows = returned_ref[:, q].reshape(targets * per_target, quarter)
        mixed = sum(jnp.dot(part, rows, preferred_element_type=F32) for part in shares)
        out_ref[:, q * quarter : (q + 1) * quarter] = mixed.astype(BF16)


def moment_kernel(
    me_ref, rows_ref, h0, h1, h2, h3, g0, g1, g2, g3, up_hbm, down_hbm, out_ref, up_ref, down_ref, sems
):
    copies = fetch([(up_hbm, up_ref), (down_hbm, down_ref)], sems)
    hiddens, pre_grads = (h0, h1, h2, h3), (g0, g1, g2, g3)
    me = me_ref[0]
    features, hidden_count = up_ref.shape
    over_rows = (((0,), (0,)), ((), ()))
    up_grad = jnp.zeros((features, hidden_count), F32)
    down_grad = jnp.zeros((hidden_count, features), F32)
    for j in range(4):
        rows = rows_ref[me ^ j].reshape(hiddens[j].shape[0], 2 * features)
        up_grad = up_grad + lax.dot_general(
            rows[:, :features],
            pre_grads[j][...],
            over_rows,
            preferred_element_type=F32,
        )
        down_grad = down_grad + lax.dot_general(
            hiddens[j][...],
            rows[:, features:],
            over_rows,
            preferred_element_type=F32,
        )
    rest = 1.0 - MOMENT_DECAY
    for copy in copies:
        copy.wait()
    up = (MOMENT_DECAY * up_ref[...].astype(F32) + rest * up_grad).astype(BF16)
    down = (MOMENT_DECAY * down_ref[...].astype(F32) + rest * down_grad).astype(BF16)
    up = up.reshape(32, 16, hidden_count)
    for j in range(2):
        for c in range(3):
            at = j * 384 + c * 128
            out_ref[j * 32 : (j + 1) * 32, c * 16 : (c + 1) * 16, :] = up[:, :, at : at + 128]
    down = down.reshape(16, 48, features)
    for j in range(4):
        out_ref[64 + j * 16 : 80 + j * 16] = down[:, :, j * 128 : (j + 1) * 128]


def pick_kernel(partner_ref, spread_ref, out_ref):
    def step(slot, carry):
        out_ref[slot] = spread_ref[partner_ref[slot]]
        return carry

    lax.fori_loop(0, out_ref.shape[0], step, 0, unroll=8)


def unpack_kernel(pieces_ref, up_ref, down_ref):
    for j in range(2):
        for c in range(3):
            at = j * 384 + c * 128
            part = pieces_ref[j * 32 : (j + 1) * 32, c * 16 : (c + 1) * 16, :]
            up_ref[:, at : at + 128] = part.reshape(512, 128)
    for j in range(4):
        part = pieces_ref[64 + j * 16 : 80 + j * 16]
        down_ref[:, j * 128 : (j + 1) * 128] = part.reshape(768, 128)


def shape_of(dims, dtype=BF16):
    return jax.ShapeDtypeStruct(dims, dtype)


def body(
    tokens,
    expert_ids,
    route_weight,
    cotangent,
    holder,
    partner,
    up_weight,
    down_weight,
    up_moment,
    down_moment,
):
    plane = lax.axis_index("zh").reshape(1).astype(jnp.int32)
    me = lax.axis_index(DP_AXES).reshape(1).astype(jnp.int32)

    packed = call(pack_kernel, "pack", shape_of((24, 4224)), [VMEM] * 5, 10**6, 4 * 10**5)(
        tokens, cotangent, expert_ids.T, route_weight.T, holder.reshape(1, -1)
    )
    gathered = lax.all_gather(packed, "zh", axis=0, tiled=True)

    up0, down0 = up_weight[0], down_weight[0]
    up2, down2 = lax.ppermute(up0, "yl", FLIP), lax.ppermute(down0, "yl", FLIP)
    up1, down1 = lax.ppermute(up0, "core", FLIP), lax.ppermute(down0, "core", FLIP)
    up3, down3 = lax.ppermute(up2, "core", FLIP), lax.ppermute(down2, "core", FLIP)
    gathered, up1, up2, up3, down1, down2, down3 = lax.optimization_barrier(
        (gathered, up1, up2, up3, down1, down2, down3)
    )
    ups, downs = (up0, up1, up2, up3), (down0, down1, down2, down3)

    outgoing, share = call(
        select_kernel,
        "select",
        (shape_of((16, 4, 16, 1024)), shape_of((192, 256), F32)),
        [SMEM, VMEM],
        10**9,
        4 * 10**6,
    )(plane, gathered)
    rows = lax.all_to_all(outgoing, GROUP_AXES, split_axis=0, concat_axis=0, tiled=True)
    by_feature = lax.all_to_all(
        rows.transpose(1, 0, 2, 3), DP_AXES, split_axis=0, concat_axis=0, tiled=True
    )

    hidden, pre_grad = call(
        forward_kernel,
        "forward",
        (shape_of((256, 768)), shape_of((256, 768))),
        [SMEM, VMEM] + [HBM] * 8,
        16 * 10**8,
        9 * 10**6,
        (
            pltpu.VMEM((4, 512, 768), BF16),
            pltpu.VMEM((4, 768, 512), BF16),
            pltpu.SemaphoreType.DMA((8,)),
        ),
    )(me, rows, *ups, *downs)
    hidden2 = lax.ppermute(hidden, "yl", FLIP)
    hidden1 = lax.ppermute(hidden, "core", FLIP)
    pre_grad1 = lax.ppermute(pre_grad, "core", FLIP)
    pre_grad2 = lax.ppermute(pre_grad, "yl", FLIP)

    expert_out = call(
        expert_out_kernel,
        "expert_out",
        shape_of((16, 4, 16, 512)),
        [SMEM, VMEM] + [HBM] * 4,
        8 * 10**8,
        5 * 10**6,
        (pltpu.VMEM((4, 768, 512), BF16), pltpu.SemaphoreType.DMA((4,))),
    )(me, hidden, *downs)

    by_feature, hidden1, hidden2, pre_grad1, expert_out = lax.optimization_barrier(
        (by_feature, hidden1, hidden2, pre_grad1, expert_out)
    )
    hidden3 = lax.ppermute(hidden2, "core", FLIP)
    pre_grad2, hidden3 = lax.optimization_barrier((pre_grad2, hidden3))
    pre_grad3 = lax.ppermute(pre_grad2, "core", FLIP)
    returned = lax.all_to_all(expert_out, GROUP_AXES, split_axis=0, concat_axis=0, tiled=True)
    partial = call(
        combine_kernel, "combine", shape_of((192, 2048)), [VMEM, VMEM], 6 * 10**8, 2 * 10**6, (), 12
    )(share, returned)
    pieces = call(
        moment_kernel,
        "moments",
        shape_of((128, 48, 128)),
        [SMEM] + [VMEM] * 9 + [HBM] * 2,
        32 * 10**8,
        9 * 10**6,
        (
            pltpu.VMEM((512, 768), BF16),
            pltpu.VMEM((768, 512), BF16),
            pltpu.SemaphoreType.DMA((2,)),
        ),
        44,
    )(
        me,
        by_feature,
        hidden,
        hidden1,
        hidden2,
        hidden3,
        pre_grad,
        pre_grad1,
        pre_grad2,
        pre_grad3,
        up_moment[0],
        down_moment[0],
    )

    layer_out = lax.psum_scatter(partial, "zh", scatter_dimension=0, tiled=True)

    spread = lax.all_to_all(pieces, SLOT_AXES, split_axis=0, concat_axis=0, tiled=True)
    spread, layer_out = lax.optimization_barrier((spread, layer_out))
    chosen = call(
        pick_kernel, "pick", shape_of((128, 48, 128)), [SMEM, VMEM], 0, 3 * 10**6, (), 12
    )(partner, spread)
    landed = lax.all_to_all(chosen, SLOT_AXES, split_axis=0, concat_axis=0, tiled=True)
    new_up, new_down = call(
        unpack_kernel,
        "unpack",
        (shape_of((512, 768)), shape_of((768, 512))),
        [VMEM],
        0,
        3 * 10**6,
        (),
        12,
    )(landed)
    return layer_out, new_up[None], new_down[None]


def solution(mesh):
    wide = Mesh(mesh.devices.reshape(2, 8, 2, 4, 2, 2), AXES)
    return jax.shard_map(
        body,
        mesh=wide,
        in_specs=(
            P(AXES, None),
            P(AXES, None),
            P(AXES, None),
            P(AXES, None),
            P(),
            P(),
            P(SLOT_AXES, DP_AXES, None),
            P(SLOT_AXES, None, DP_AXES),
            P(SLOT_AXES, DP_AXES, None),
            P(SLOT_AXES, None, DP_AXES),
        ),
        out_specs=(
            P(AXES, None),
            P(SLOT_AXES, DP_AXES, None),
            P(SLOT_AXES, None, DP_AXES),
        ),
        check_vma=False,
    )
```

```python
import jax
import jax.numpy as jnp
from jax import lax
from jax.experimental import pallas as pl
from jax.experimental.pallas import tpu as pltpu
from jax.sharding import Mesh, PartitionSpec as P

MOMENT_DECAY = 0.9
GATHERED_COTS = 640
AXES = ("yh", "zh", "zp", "x", "yl", "core")
SLOT_AXES = ("yh", "zh", "zp", "x")
GROUP_AXES = ("yh", "zp", "x")
DP_AXES = ("yl", "core")
BF16 = jnp.bfloat16
F32 = jnp.float32
FLIP = [(0, 1), (1, 0)]
VMEM = pl.BlockSpec(memory_space=pltpu.VMEM)
SMEM = pl.BlockSpec(memory_space=pltpu.SMEM)
HBM = pl.BlockSpec(memory_space=pltpu.HBM)


def call(kernel, name, out_shape, in_specs, flops, moved, scratch=(), grant=62):
    outs = jax.tree.map(lambda _: VMEM, out_shape)
    return pl.pallas_call(
        kernel,
        name=name,
        out_shape=out_shape,
        in_specs=in_specs,
        out_specs=outs,
        scratch_shapes=scratch,
        compiler_params=pltpu.CompilerParams(vmem_limit_bytes=grant * 1024 * 1024),
        cost_estimate=pl.CostEstimate(flops=flops, bytes_accessed=moved, transcendentals=0),
    )


def split3(value):
    high = value.astype(BF16)
    rest = value - high.astype(F32)
    middle = rest.astype(BF16)
    low = (rest - middle.astype(F32)).astype(BF16)
    return high, middle, low


def fetch(pairs, sems):
    copies = [
        pltpu.make_async_copy(source, target, sems.at[i]) for i, (source, target) in enumerate(pairs)
    ]
    for copy in copies:
        copy.start()
    return copies


def pack_kernel(tok_ref, cot_ref, ids_ref, weight_ref, holder_ref, out_ref):
    top, rows = ids_ref.shape
    width = tok_ref.shape[1]
    experts = holder_ref.shape[1]
    row_at = lax.broadcasted_iota(jnp.int32, (rows, rows), 0)
    column_at = lax.broadcasted_iota(jnp.int32, (rows, rows), 1)
    same = (row_at == column_at).astype(BF16)

    def turned(value):
        return lax.dot_general(
            same, value.astype(BF16), (((1,), (1,)), ((), ())), preferred_element_type=F32
        )

    ids = turned(ids_ref[...].astype(F32))
    parts = [turned(part) for part in split3(weight_ref[...])]
    lane = lax.broadcasted_iota(jnp.int32, (rows, experts), 1).astype(F32)
    hits = [(ids[:, k : k + 1] == lane).astype(F32) for k in range(top)]
    hit = sum(hits[1:], hits[0])
    earlier = (row_at > column_at).astype(BF16)
    before = jnp.dot(earlier, hit.astype(BF16), preferred_element_type=F32)
    base = 2.0 * holder_ref[...].astype(F32) + before
    meta_lane = lax.broadcasted_iota(jnp.int32, (rows, 128), 1)
    meta = jnp.zeros((rows, 128), F32)
    for k in range(top):
        code = jnp.sum(hits[k] * base, axis=1, keepdims=True)
        meta = jnp.where(meta_lane == k, code, meta)
        for place, part in enumerate(parts):
            meta = jnp.where(meta_lane == (place + 1) * top + k, part[:, k : k + 1], meta)
    out_ref[:, :width] = tok_ref[...]
    out_ref[:, width : width + 128] = meta.astype(BF16)
    out_ref[:, width + 128 :] = cot_ref[:, :GATHERED_COTS]


def select_kernel(plane_ref, gathered_ref, cots_ref, out_ref, share_ref):
    total = gathered_ref.shape[0]
    targets, quarters, per_target, _ = out_ref.shape
    quarter = out_ref.shape[3] // 2
    width = quarters * quarter
    top = 8
    rows = targets * per_target
    block = total // (per_target // 2)
    plane = plane_ref[0]
    meta = gathered_ref[:, width : width + 128].astype(F32)
    row = lax.broadcasted_iota(jnp.int32, (total, rows), 1)
    token = lax.broadcasted_iota(jnp.int32, (total, rows), 0)
    target = row >> 4
    first = ((row >> 1) & 7) * block
    inside = (token >= first) & (token < first + block)
    slot = (target >> 3) * 64 + plane * 8 + (target & 7)
    wanted = jnp.where(inside, slot * 2 + (row & 1), -1).astype(F32)
    picked = jnp.zeros((total, rows), F32)
    share = jnp.zeros((total, rows), F32)
    for k in range(top):
        match = meta[:, k : k + 1] == wanted
        weight = (
            meta[:, top + k : top + k + 1]
            + meta[:, 2 * top + k : 2 * top + k + 1]
            + meta[:, 3 * top + k : 3 * top + k + 1]
        )
        picked = jnp.where(match, 1.0, picked)
        share = jnp.where(match, weight, share)
    share_ref[...] = share
    picked_t = jnp.transpose(picked).astype(BF16)
    shares_t = split3(jnp.transpose(share))
    for q in range(quarters):
        at = q * quarter
        sent = jnp.dot(
            picked_t, gathered_ref[:, at : at + quarter], preferred_element_type=F32
        ).astype(BF16)
        out_ref[:, q, :, :quarter] = sent.reshape(targets, per_target, quarter)
        cut = min(max(GATHERED_COTS - at, 0), quarter)
        near = gathered_ref[:, width + 128 + at : width + 128 + at + cut] if cut else None
        far = cots_ref[:, at + cut - GATHERED_COTS : at + quarter - GATHERED_COTS] if cut < quarter else None
        cot = near if far is None else far if near is None else jnp.concatenate([near, far], axis=1)
        grads = sum(jnp.dot(part, cot, preferred_element_type=F32) for part in shares_t)
        out_ref[:, q, :, quarter:] = grads.astype(BF16).reshape(targets, per_target, quarter)


def forward_kernel(me_ref, rows_ref, *refs):
    sources, out_ref, ups, downs, sems = refs[:8], refs[8], refs[9], refs[10], refs[11]
    copies = fetch(
        [(sources[j + 4 * kind], held.at[j]) for j in range(4) for kind, held in ((0, ups), (1, downs))],
        sems,
    )
    targets, _, per_target, double = rows_ref.shape
    quarter = double // 2
    count = targets * per_target
    hidden_count = ups.shape[2]
    me = me_ref[0]
    preact = jnp.zeros((count, hidden_count), F32)
    back = jnp.zeros((count, hidden_count), F32)
    for j in range(4):
        both = rows_ref[:, me ^ j].reshape(count, double)
        copies[2 * j].wait()
        preact = preact + jnp.dot(both[:, :quarter], ups[j], preferred_element_type=F32)
        copies[2 * j + 1].wait()
        back = back + lax.dot_general(
            both[:, quarter:], downs[j], (((1,), (1,)), ((), ())), preferred_element_type=F32
        )
    sigmoid = 1.0 / (1.0 + jnp.exp(-preact))
    out_ref[:, :hidden_count] = (preact * sigmoid).astype(BF16)
    out_ref[:, hidden_count:] = (back * sigmoid * (1.0 + preact * (1.0 - sigmoid))).astype(BF16)


def expert_out_kernel(me_ref, acts_ref, *refs):
    sources, out_ref, downs, sems = refs[:4], refs[4], refs[5], refs[6]
    copies = fetch([(sources[j], downs.at[j]) for j in range(4)], sems)
    targets, _, per_target, quarter = out_ref.shape
    hidden = acts_ref[:, : downs.shape[1]]
    me = me_ref[0]
    for j in range(4):
        copies[j].wait()
        part = jnp.dot(hidden, downs[j], preferred_element_type=F32).astype(BF16)
        out_ref[:, me ^ j] = part.reshape(targets, per_target, quarter)


def combine_kernel(share_ref, returned_ref, out_ref):
    targets, quarters, per_target, quarter = returned_ref.shape
    shares = split3(share_ref[...])
    for q in range(quarters):
        rows = returned_ref[:, q].reshape(targets * per_target, quarter)
        mixed = sum(jnp.dot(part, rows, preferred_element_type=F32) for part in shares)
        out_ref[:, q * quarter : (q + 1) * quarter] = mixed.astype(BF16)


def moment_kernel(
    me_ref, rows_ref, a0, a1, a2, a3, up_hbm, down_hbm, out_ref, up_ref, down_ref, sems
):
    copies = fetch([(up_hbm, up_ref), (down_hbm, down_ref)], sems)
    acts = (a0, a1, a2, a3)
    me = me_ref[0]
    features, hidden_count = up_ref.shape
    over_rows = (((0,), (0,)), ((), ()))
    up_grad = jnp.zeros((features, hidden_count), F32)
    down_grad = jnp.zeros((hidden_count, features), F32)
    for j in range(4):
        rows = rows_ref[me ^ j].reshape(acts[j].shape[0], 2 * features)
        up_grad = up_grad + lax.dot_general(
            rows[:, :features],
            acts[j][:, hidden_count:],
            over_rows,
            preferred_element_type=F32,
        )
        down_grad = down_grad + lax.dot_general(
            acts[j][:, :hidden_count],
            rows[:, features:],
            over_rows,
            preferred_element_type=F32,
        )
    rest = 1.0 - MOMENT_DECAY
    for copy in copies:
        copy.wait()
    up = (MOMENT_DECAY * up_ref[...].astype(F32) + rest * up_grad).astype(BF16)
    down = (MOMENT_DECAY * down_ref[...].astype(F32) + rest * down_grad).astype(BF16)
    up = up.reshape(32, 16, hidden_count)
    for j in range(2):
        for c in range(3):
            at = j * 384 + c * 128
            out_ref[j * 32 : (j + 1) * 32, c * 16 : (c + 1) * 16, :] = up[:, :, at : at + 128]
    down = down.reshape(16, 48, features)
    for j in range(4):
        out_ref[64 + j * 16 : 80 + j * 16] = down[:, :, j * 128 : (j + 1) * 128]


def pick_kernel(partner_ref, spread_ref, out_ref):
    def step(slot, carry):
        out_ref[slot] = spread_ref[partner_ref[slot]]
        return carry

    lax.fori_loop(0, out_ref.shape[0], step, 0, unroll=8)


def unpack_kernel(pieces_ref, up_ref, down_ref):
    for j in range(2):
        for c in range(3):
            at = j * 384 + c * 128
            part = pieces_ref[j * 32 : (j + 1) * 32, c * 16 : (c + 1) * 16, :]
            up_ref[:, at : at + 128] = part.reshape(512, 128)
    for j in range(4):
        part = pieces_ref[64 + j * 16 : 80 + j * 16]
        down_ref[:, j * 128 : (j + 1) * 128] = part.reshape(768, 128)


def shape_of(dims, dtype=BF16):
    return jax.ShapeDtypeStruct(dims, dtype)


def body(
    tokens,
    expert_ids,
    route_weight,
    cotangent,
    holder,
    partner,
    up_weight,
    down_weight,
    up_moment,
    down_moment,
):
    plane = lax.axis_index("zh").reshape(1).astype(jnp.int32)
    me = lax.axis_index(DP_AXES).reshape(1).astype(jnp.int32)

    packed = call(pack_kernel, "pack", shape_of((24, 2816)), [VMEM] * 5, 10**6, 2 * 10**5)(
        tokens, cotangent, expert_ids.T, route_weight.T, holder.reshape(1, -1)
    )
    rest = cotangent[:, GATHERED_COTS:]
    copies = jnp.broadcast_to(rest[None], (8,) + rest.shape)
    packed, copies, up0, down0 = lax.optimization_barrier(
        (packed, copies, up_weight[0], down_weight[0])
    )
    gathered = lax.all_gather(packed, "zh", axis=0, tiled=True)
    cots = lax.all_to_all(copies, "zh", split_axis=0, concat_axis=0, tiled=True).reshape(192, -1)

    up2, down2 = lax.ppermute(up0, "yl", FLIP), lax.ppermute(down0, "yl", FLIP)
    up1, down1 = lax.ppermute(up0, "core", FLIP), lax.ppermute(down0, "core", FLIP)
    up3, down3 = lax.ppermute(up2, "core", FLIP), lax.ppermute(down2, "core", FLIP)
    gathered, cots, up1, up2, up3, down1, down2, down3 = lax.optimization_barrier(
        (gathered, cots, up1, up2, up3, down1, down2, down3)
    )
    ups, downs = (up0, up1, up2, up3), (down0, down1, down2, down3)

    outgoing, share = call(
        select_kernel,
        "select",
        (shape_of((16, 4, 16, 1024)), shape_of((192, 256), F32)),
        [SMEM, VMEM, VMEM],
        10**9,
        4 * 10**6,
    )(plane, gathered, cots)
    rows = lax.all_to_all(outgoing, GROUP_AXES, split_axis=0, concat_axis=0, tiled=True)
    by_feature = lax.all_to_all(
        rows.transpose(1, 0, 2, 3), DP_AXES, split_axis=0, concat_axis=0, tiled=True
    )

    acts = call(
        forward_kernel,
        "forward",
        shape_of((256, 1536)),
        [SMEM, VMEM] + [HBM] * 8,
        16 * 10**8,
        9 * 10**6,
        (
            pltpu.VMEM((4, 512, 768), BF16),
            pltpu.VMEM((4, 768, 512), BF16),
            pltpu.SemaphoreType.DMA((8,)),
        ),
    )(me, rows, *ups, *downs)
    acts2 = lax.ppermute(acts, "yl", FLIP)
    acts1 = lax.ppermute(acts, "core", FLIP)

    expert_out = call(
        expert_out_kernel,
        "expert_out",
        shape_of((16, 4, 16, 512)),
        [SMEM, VMEM] + [HBM] * 4,
        8 * 10**8,
        5 * 10**6,
        (pltpu.VMEM((4, 768, 512), BF16), pltpu.SemaphoreType.DMA((4,))),
    )(me, acts, *downs)

    by_feature, acts1, acts2, expert_out = lax.optimization_barrier(
        (by_feature, acts1, acts2, expert_out)
    )
    acts3 = lax.ppermute(acts2, "core", FLIP)
    returned = lax.all_to_all(expert_out, GROUP_AXES, split_axis=0, concat_axis=0, tiled=True)
    partial = call(
        combine_kernel, "combine", shape_of((192, 2048)), [VMEM, VMEM], 6 * 10**8, 2 * 10**6, (), 12
    )(share, returned)
    pieces = call(
        moment_kernel,
        "moments",
        shape_of((128, 48, 128)),
        [SMEM] + [VMEM] * 5 + [HBM] * 2,
        32 * 10**8,
        9 * 10**6,
        (
            pltpu.VMEM((512, 768), BF16),
            pltpu.VMEM((768, 512), BF16),
            pltpu.SemaphoreType.DMA((2,)),
        ),
    )(me, by_feature, acts, acts1, acts2, acts3, up_moment[0], down_moment[0])

    layer_out = lax.psum_scatter(partial, "zh", scatter_dimension=0, tiled=True)

    spread = lax.all_to_all(pieces, SLOT_AXES, split_axis=0, concat_axis=0, tiled=True)
    spread, layer_out = lax.optimization_barrier((spread, layer_out))
    chosen = call(
        pick_kernel, "pick", shape_of((128, 48, 128)), [SMEM, VMEM], 0, 3 * 10**6, (), 12
    )(partner, spread)
    landed = lax.all_to_all(chosen, SLOT_AXES, split_axis=0, concat_axis=0, tiled=True)
    new_up, new_down = call(
        unpack_kernel,
        "unpack",
        (shape_of((512, 768)), shape_of((768, 512))),
        [VMEM],
        0,
        3 * 10**6,
        (),
        12,
    )(landed)
    return layer_out, new_up[None], new_down[None]


def solution(mesh):
    wide = Mesh(mesh.devices.reshape(2, 8, 2, 4, 2, 2), AXES)
    return jax.shard_map(
        body,
        mesh=wide,
        in_specs=(
            P(AXES, None),
            P(AXES, None),
            P(AXES, None),
            P(AXES, None),
            P(),
            P(),
            P(SLOT_AXES, DP_AXES, None),
            P(SLOT_AXES, None, DP_AXES),
            P(SLOT_AXES, DP_AXES, None),
            P(SLOT_AXES, None, DP_AXES),
        ),
        out_specs=(
            P(AXES, None),
            P(SLOT_AXES, DP_AXES, None),
            P(SLOT_AXES, None, DP_AXES),
        ),
        check_vma=False,
    )
```

```python
import jax
import jax.numpy as jnp
from jax import lax
from jax.experimental import pallas as pl
from jax.experimental.pallas import tpu as pltpu
from jax.sharding import Mesh, PartitionSpec as P

MOMENT_DECAY = 0.9
AXES = ("yh", "zh", "zp", "x", "yl", "core")
SLOT_AXES = ("yh", "zh", "zp", "x")
GROUP_AXES = ("yh", "zp", "x")
DP_AXES = ("yl", "core")
BF16 = jnp.bfloat16
F32 = jnp.float32
FLIP = [(0, 1), (1, 0)]
VMEM = pl.BlockSpec(memory_space=pltpu.VMEM)
SMEM = pl.BlockSpec(memory_space=pltpu.SMEM)
HBM = pl.BlockSpec(memory_space=pltpu.HBM)


def call(kernel, name, out_shape, in_specs, flops, moved, scratch=(), grant=62):
    outs = jax.tree.map(lambda _: VMEM, out_shape)
    return pl.pallas_call(
        kernel,
        name=name,
        out_shape=out_shape,
        in_specs=in_specs,
        out_specs=outs,
        scratch_shapes=scratch,
        compiler_params=pltpu.CompilerParams(vmem_limit_bytes=grant * 1024 * 1024),
        cost_estimate=pl.CostEstimate(flops=flops, bytes_accessed=moved, transcendentals=0),
    )


def split3(value):
    high = value.astype(BF16)
    rest = value - high.astype(F32)
    middle = rest.astype(BF16)
    low = (rest - middle.astype(F32)).astype(BF16)
    return high, middle, low


def fetch(pairs, sems):
    copies = [
        pltpu.make_async_copy(source, target, sems.at[i]) for i, (source, target) in enumerate(pairs)
    ]
    for copy in copies:
        copy.start()
    return copies


def pack_kernel(tok_ref, cot_ref, ids_ref, weight_ref, holder_ref, out_ref):
    top, rows = ids_ref.shape
    width = tok_ref.shape[1]
    experts = holder_ref.shape[1]
    row_at = lax.broadcasted_iota(jnp.int32, (rows, rows), 0)
    column_at = lax.broadcasted_iota(jnp.int32, (rows, rows), 1)
    same = (row_at == column_at).astype(BF16)

    def turned(value):
        return lax.dot_general(
            same, value.astype(BF16), (((1,), (1,)), ((), ())), preferred_element_type=F32
        )

    ids = turned(ids_ref[...].astype(F32))
    parts = [turned(part) for part in split3(weight_ref[...])]
    lane = lax.broadcasted_iota(jnp.int32, (rows, experts), 1).astype(F32)
    hits = [(ids[:, k : k + 1] == lane).astype(F32) for k in range(top)]
    hit = sum(hits[1:], hits[0])
    earlier = (row_at > column_at).astype(BF16)
    before = jnp.dot(earlier, hit.astype(BF16), preferred_element_type=F32)
    base = 2.0 * holder_ref[...].astype(F32) + before
    meta_lane = lax.broadcasted_iota(jnp.int32, (rows, 128), 1)
    meta = jnp.zeros((rows, 128), F32)
    for k in range(top):
        code = jnp.sum(hits[k] * base, axis=1, keepdims=True)
        meta = jnp.where(meta_lane == k, code, meta)
        for place, part in enumerate(parts):
            meta = jnp.where(meta_lane == (place + 1) * top + k, part[:, k : k + 1], meta)
    out_ref[:, :width] = tok_ref[...]
    out_ref[:, width : 2 * width] = cot_ref[...]
    out_ref[:, 2 * width :] = meta.astype(BF16)


def select_kernel(plane_ref, gathered_ref, out_ref, share_ref):
    total = gathered_ref.shape[0]
    targets, quarters, per_target, _ = out_ref.shape
    quarter = out_ref.shape[3] // 2
    width = quarters * quarter
    top = 8
    rows = targets * per_target
    block = total // (per_target // 2)
    plane = plane_ref[0]
    meta = gathered_ref[:, 2 * width :].astype(F32)
    row = lax.broadcasted_iota(jnp.int32, (total, rows), 1)
    token = lax.broadcasted_iota(jnp.int32, (total, rows), 0)
    target = row >> 4
    first = ((row >> 1) & 7) * block
    inside = (token >= first) & (token < first + block)
    slot = (target >> 3) * 64 + plane * 8 + (target & 7)
    wanted = jnp.where(inside, slot * 2 + (row & 1), -1).astype(F32)
    picked = jnp.zeros((total, rows), F32)
    share = jnp.zeros((total, rows), F32)
    for k in range(top):
        match = meta[:, k : k + 1] == wanted
        weight = (
            meta[:, top + k : top + k + 1]
            + meta[:, 2 * top + k : 2 * top + k + 1]
            + meta[:, 3 * top + k : 3 * top + k + 1]
        )
        picked = jnp.where(match, 1.0, picked)
        share = jnp.where(match, weight, share)
    share_ref[...] = share
    picked_t = jnp.transpose(picked).astype(BF16)
    shares_t = split3(jnp.transpose(share))
    for q in range(quarters):
        at = q * quarter
        sent = jnp.dot(
            picked_t, gathered_ref[:, at : at + quarter], preferred_element_type=F32
        ).astype(BF16)
        out_ref[:, q, :, :quarter] = sent.reshape(targets, per_target, quarter)
        cot = gathered_ref[:, width + at : width + at + quarter]
        grads = sum(jnp.dot(part, cot, preferred_element_type=F32) for part in shares_t)
        out_ref[:, q, :, quarter:] = grads.astype(BF16).reshape(targets, per_target, quarter)


def forward_kernel(me_ref, rows_ref, *refs):
    sources, out_ref, sent_ref, ups, downs, sems = refs[:8], *refs[8:]
    copies = fetch(
        [(sources[j], ups.at[j]) for j in range(4)]
        + [(sources[4 + j], downs.at[j]) for j in range(4)],
        sems,
    )
    targets, _, per_target, double = rows_ref.shape
    quarter = double // 2
    count = targets * per_target
    hidden_count = ups.shape[2]
    me = me_ref[0]
    preact = jnp.zeros((count, hidden_count), F32)
    for j in range(4):
        tok = rows_ref[:, me ^ j, :, :quarter].reshape(count, quarter)
        copies[j].wait()
        preact = preact + jnp.dot(tok, ups[j], preferred_element_type=F32)
    sigmoid = 1.0 / (1.0 + jnp.exp(-preact))
    hidden = (preact * sigmoid).astype(BF16)
    slope = sigmoid * (1.0 + preact * (1.0 - sigmoid))
    out_ref[:, :hidden_count] = hidden
    back = jnp.zeros((count, hidden_count), F32)
    for j in range(4):
        grad = rows_ref[:, me ^ j, :, quarter:].reshape(count, quarter)
        copies[4 + j].wait()
        back = back + lax.dot_general(
            grad, downs[j], (((1,), (1,)), ((), ())), preferred_element_type=F32
        )
    out_ref[:, hidden_count:] = (back * slope).astype(BF16)
    for j in range(4):
        part = jnp.dot(hidden, downs[j], preferred_element_type=F32).astype(BF16)
        sent_ref[:, me ^ j] = part.reshape(targets, per_target, quarter)


def combine_kernel(share_ref, returned_ref, out_ref):
    targets, quarters, per_target, quarter = returned_ref.shape
    shares = split3(share_ref[...])
    for q in range(quarters):
        rows = returned_ref[:, q].reshape(targets * per_target, quarter)
        mixed = sum(jnp.dot(part, rows, preferred_element_type=F32) for part in shares)
        out_ref[:, q * quarter : (q + 1) * quarter] = mixed.astype(BF16)


def moment_kernel(
    me_ref, rows_ref, a0, a1, a2, a3, up_hbm, down_hbm, out_ref, up_ref, down_ref, sems
):
    copies = fetch([(up_hbm, up_ref), (down_hbm, down_ref)], sems)
    acts = (a0, a1, a2, a3)
    me = me_ref[0]
    features, hidden_count = up_ref.shape
    over_rows = (((0,), (0,)), ((), ()))
    up_grad = jnp.zeros((features, hidden_count), F32)
    down_grad = jnp.zeros((hidden_count, features), F32)
    for j in range(4):
        rows = rows_ref[me ^ j].reshape(acts[j].shape[0], 2 * features)
        up_grad = up_grad + lax.dot_general(
            rows[:, :features],
            acts[j][:, hidden_count:],
            over_rows,
            preferred_element_type=F32,
        )
        down_grad = down_grad + lax.dot_general(
            acts[j][:, :hidden_count],
            rows[:, features:],
            over_rows,
            preferred_element_type=F32,
        )
    rest = 1.0 - MOMENT_DECAY
    for copy in copies:
        copy.wait()
    up = (MOMENT_DECAY * up_ref[...].astype(F32) + rest * up_grad).astype(BF16)
    down = (MOMENT_DECAY * down_ref[...].astype(F32) + rest * down_grad).astype(BF16)
    up = up.reshape(32, 16, hidden_count)
    for j in range(2):
        for c in range(3):
            at = j * 384 + c * 128
            out_ref[j * 32 : (j + 1) * 32, c * 16 : (c + 1) * 16, :] = up[:, :, at : at + 128]
    down = down.reshape(16, 48, features)
    for j in range(4):
        out_ref[64 + j * 16 : 80 + j * 16] = down[:, :, j * 128 : (j + 1) * 128]


def pick_kernel(partner_ref, spread_ref, out_ref):
    def step(slot, carry):
        out_ref[slot] = spread_ref[partner_ref[slot]]
        return carry

    lax.fori_loop(0, out_ref.shape[0], step, 0, unroll=8)


def unpack_kernel(pieces_ref, up_ref, down_ref):
    for j in range(2):
        for c in range(3):
            at = j * 384 + c * 128
            part = pieces_ref[j * 32 : (j + 1) * 32, c * 16 : (c + 1) * 16, :]
            up_ref[:, at : at + 128] = part.reshape(512, 128)
    for j in range(4):
        part = pieces_ref[64 + j * 16 : 80 + j * 16]
        down_ref[:, j * 128 : (j + 1) * 128] = part.reshape(768, 128)


def shape_of(dims, dtype=BF16):
    return jax.ShapeDtypeStruct(dims, dtype)


def body(
    tokens,
    expert_ids,
    route_weight,
    cotangent,
    holder,
    partner,
    up_weight,
    down_weight,
    up_moment,
    down_moment,
):
    plane = lax.axis_index("zh").reshape(1).astype(jnp.int32)
    me = lax.axis_index(DP_AXES).reshape(1).astype(jnp.int32)

    packed = call(pack_kernel, "pack", shape_of((24, 4224)), [VMEM] * 5, 10**6, 4 * 10**5)(
        tokens, cotangent, expert_ids.T, route_weight.T, holder.reshape(1, -1)
    )
    gathered = lax.all_gather(packed, "zh", axis=0, tiled=True)

    up0, down0 = up_weight[0], down_weight[0]
    up2, down2 = lax.ppermute(up0, "yl", FLIP), lax.ppermute(down0, "yl", FLIP)
    up1, down1 = lax.ppermute(up0, "core", FLIP), lax.ppermute(down0, "core", FLIP)
    up3, down3 = lax.ppermute(up2, "core", FLIP), lax.ppermute(down2, "core", FLIP)
    gathered, up1, up2, up3, down1, down2, down3 = lax.optimization_barrier(
        (gathered, up1, up2, up3, down1, down2, down3)
    )
    ups, downs = (up0, up1, up2, up3), (down0, down1, down2, down3)

    outgoing, share = call(
        select_kernel,
        "select",
        (shape_of((16, 4, 16, 1024)), shape_of((192, 256), F32)),
        [SMEM, VMEM],
        10**9,
        4 * 10**6,
    )(plane, gathered)
    rows = lax.all_to_all(outgoing, GROUP_AXES, split_axis=0, concat_axis=0, tiled=True)

    acts, expert_out = call(
        forward_kernel,
        "forward",
        (shape_of((256, 1536)), shape_of((16, 4, 16, 512))),
        [SMEM, VMEM] + [HBM] * 8,
        24 * 10**8,
        10**7,
        (
            pltpu.VMEM((4, 512, 768), BF16),
            pltpu.VMEM((4, 768, 512), BF16),
            pltpu.SemaphoreType.DMA((8,)),
        ),
    )(me, rows, *ups, *downs)
    acts2 = lax.ppermute(acts, "yl", FLIP)
    acts1 = lax.ppermute(acts, "core", FLIP)

    returned = lax.all_to_all(expert_out, GROUP_AXES, split_axis=0, concat_axis=0, tiled=True)
    turned_rows, returned, acts1 = lax.optimization_barrier(
        (rows.transpose(1, 0, 2, 3), returned, acts1)
    )
    by_feature = lax.all_to_all(turned_rows, DP_AXES, split_axis=0, concat_axis=0, tiled=True)
    acts3 = lax.ppermute(acts2, "core", FLIP)
    partial = call(
        combine_kernel, "combine", shape_of((192, 2048)), [VMEM, VMEM], 6 * 10**8, 2 * 10**6, (), 12
    )(share, returned)
    layer_out = lax.psum_scatter(partial, "zh", scatter_dimension=0, tiled=True)

    pieces = call(
        moment_kernel,
        "moments",
        shape_of((128, 48, 128)),
        [SMEM] + [VMEM] * 5 + [HBM] * 2,
        32 * 10**8,
        9 * 10**6,
        (
            pltpu.VMEM((512, 768), BF16),
            pltpu.VMEM((768, 512), BF16),
            pltpu.SemaphoreType.DMA((2,)),
        ),
    )(me, by_feature, acts, acts1, acts2, acts3, up_moment[0], down_moment[0])


    pieces, layer_out = lax.optimization_barrier((pieces, layer_out))
    spread = lax.all_to_all(pieces, SLOT_AXES, split_axis=0, concat_axis=0, tiled=True)
    chosen = call(
        pick_kernel, "pick", shape_of((128, 48, 128)), [SMEM, VMEM], 0, 3 * 10**6, (), 12
    )(partner, spread)
    landed = lax.all_to_all(chosen, SLOT_AXES, split_axis=0, concat_axis=0, tiled=True)
    new_up, new_down = call(
        unpack_kernel,
        "unpack",
        (shape_of((512, 768)), shape_of((768, 512))),
        [VMEM],
        0,
        3 * 10**6,
        (),
        12,
    )(landed)
    return layer_out, new_up[None], new_down[None]


def solution(mesh):
    wide = Mesh(mesh.devices.reshape(2, 8, 2, 4, 2, 2), AXES)
    return jax.shard_map(
        body,
        mesh=wide,
        in_specs=(
            P(AXES, None),
            P(AXES, None),
            P(AXES, None),
            P(AXES, None),
            P(),
            P(),
            P(SLOT_AXES, DP_AXES, None),
            P(SLOT_AXES, None, DP_AXES),
            P(SLOT_AXES, DP_AXES, None),
            P(SLOT_AXES, None, DP_AXES),
        ),
        out_specs=(
            P(AXES, None),
            P(SLOT_AXES, DP_AXES, None),
            P(SLOT_AXES, None, DP_AXES),
        ),
        check_vma=False,
    )
```

```python
import jax
import jax.numpy as jnp
from jax import lax
from jax.experimental import pallas as pl
from jax.experimental.pallas import tpu as pltpu
from jax.sharding import Mesh, PartitionSpec as P

MOMENT_DECAY = 0.9
AXES = ("yh", "zh", "zp", "x", "yl", "core")
SLOT_AXES = ("yh", "zh", "zp", "x")
GROUP_AXES = ("yh", "zp", "x")
DP_AXES = ("yl", "core")
BF16 = jnp.bfloat16
F32 = jnp.float32
FLIP = [(0, 1), (1, 0)]
VMEM = pl.BlockSpec(memory_space=pltpu.VMEM)
SMEM = pl.BlockSpec(memory_space=pltpu.SMEM)
HBM = pl.BlockSpec(memory_space=pltpu.HBM)


def call(kernel, name, out_shape, in_specs, flops, moved, scratch=(), grant=62):
    outs = jax.tree.map(lambda _: VMEM, out_shape)
    return pl.pallas_call(
        kernel,
        name=name,
        out_shape=out_shape,
        in_specs=in_specs,
        out_specs=outs,
        scratch_shapes=scratch,
        compiler_params=pltpu.CompilerParams(vmem_limit_bytes=grant * 1024 * 1024),
        cost_estimate=pl.CostEstimate(flops=flops, bytes_accessed=moved, transcendentals=0),
    )


def split3(value):
    high = value.astype(BF16)
    rest = value - high.astype(F32)
    middle = rest.astype(BF16)
    low = (rest - middle.astype(F32)).astype(BF16)
    return high, middle, low


def fetch(pairs, sems):
    copies = [
        pltpu.make_async_copy(source, target, sems.at[i]) for i, (source, target) in enumerate(pairs)
    ]
    for copy in copies:
        copy.start()
    return copies


def pack_kernel(tok_ref, cot_ref, ids_ref, weight_ref, holder_ref, out_ref):
    top, rows = ids_ref.shape
    width = tok_ref.shape[1]
    experts = holder_ref.shape[1]
    row_at = lax.broadcasted_iota(jnp.int32, (rows, rows), 0)
    column_at = lax.broadcasted_iota(jnp.int32, (rows, rows), 1)
    same = (row_at == column_at).astype(BF16)

    def turned(value):
        return lax.dot_general(
            same, value.astype(BF16), (((1,), (1,)), ((), ())), preferred_element_type=F32
        )

    ids = turned(ids_ref[...].astype(F32))
    parts = [turned(part) for part in split3(weight_ref[...])]
    lane = lax.broadcasted_iota(jnp.int32, (rows, experts), 1).astype(F32)
    hits = [(ids[:, k : k + 1] == lane).astype(F32) for k in range(top)]
    hit = sum(hits[1:], hits[0])
    earlier = (row_at > column_at).astype(BF16)
    before = jnp.dot(earlier, hit.astype(BF16), preferred_element_type=F32)
    base = 2.0 * holder_ref[...].astype(F32) + before
    meta_lane = lax.broadcasted_iota(jnp.int32, (rows, 128), 1)
    meta = jnp.zeros((rows, 128), F32)
    for k in range(top):
        code = jnp.sum(hits[k] * base, axis=1, keepdims=True)
        meta = jnp.where(meta_lane == k, code, meta)
        for place, part in enumerate(parts):
            meta = jnp.where(meta_lane == (place + 1) * top + k, part[:, k : k + 1], meta)
    out_ref[:, :width] = tok_ref[...]
    out_ref[:, width : 2 * width] = cot_ref[...]
    out_ref[:, 2 * width :] = meta.astype(BF16)


def select_kernel(plane_ref, gathered_ref, out_ref, share_ref):
    total = gathered_ref.shape[0]
    targets, quarters, per_target, _ = out_ref.shape
    quarter = out_ref.shape[3] // 2
    width = quarters * quarter
    top = 8
    rows = targets * per_target
    block = total // (per_target // 2)
    plane = plane_ref[0]
    meta = gathered_ref[:, 2 * width :].astype(F32)
    row = lax.broadcasted_iota(jnp.int32, (total, rows), 1)
    token = lax.broadcasted_iota(jnp.int32, (total, rows), 0)
    target = row >> 4
    first = ((row >> 1) & 7) * block
    inside = (token >= first) & (token < first + block)
    slot = (target >> 3) * 64 + plane * 8 + (target & 7)
    wanted = jnp.where(inside, slot * 2 + (row & 1), -1).astype(F32)
    picked = jnp.zeros((total, rows), F32)
    share = jnp.zeros((total, rows), F32)
    for k in range(top):
        match = meta[:, k : k + 1] == wanted
        weight = (
            meta[:, top + k : top + k + 1]
            + meta[:, 2 * top + k : 2 * top + k + 1]
            + meta[:, 3 * top + k : 3 * top + k + 1]
        )
        picked = jnp.where(match, 1.0, picked)
        share = jnp.where(match, weight, share)
    share_ref[...] = share
    picked_t = jnp.transpose(picked).astype(BF16)
    shares_t = split3(jnp.transpose(share))
    for q in range(quarters):
        at = q * quarter
        sent = jnp.dot(
            picked_t, gathered_ref[:, at : at + quarter], preferred_element_type=F32
        ).astype(BF16)
        out_ref[:, q, :, :quarter] = sent.reshape(targets, per_target, quarter)
        cot = gathered_ref[:, width + at : width + at + quarter]
        grads = sum(jnp.dot(part, cot, preferred_element_type=F32) for part in shares_t)
        out_ref[:, q, :, quarter:] = grads.astype(BF16).reshape(targets, per_target, quarter)


def forward_kernel(me_ref, rows_ref, *refs):
    sources, hidden_ref, slope_ref, sent_ref, ups, downs, sems = refs[:8], *refs[8:]
    copies = fetch(
        [(sources[j], ups.at[j]) for j in range(4)]
        + [(sources[4 + j], downs.at[j]) for j in range(4)],
        sems,
    )
    targets, _, per_target, double = rows_ref.shape
    quarter = double // 2
    count = targets * per_target
    me = me_ref[0]
    preact = jnp.zeros((count, ups.shape[2]), F32)
    for j in range(4):
        tok = rows_ref[:, me ^ j, :, :quarter].reshape(count, quarter)
        copies[j].wait()
        preact = preact + jnp.dot(tok, ups[j], preferred_element_type=F32)
    sigmoid = 1.0 / (1.0 + jnp.exp(-preact))
    hidden = (preact * sigmoid).astype(BF16)
    hidden_ref[...] = hidden
    slope_ref[...] = sigmoid * (1.0 + preact * (1.0 - sigmoid))
    for j in range(4):
        copies[4 + j].wait()
        part = jnp.dot(hidden, downs[j], preferred_element_type=F32).astype(BF16)
        sent_ref[:, me ^ j] = part.reshape(targets, per_target, quarter)


def back_kernel(me_ref, rows_ref, hidden_ref, slope_ref, *refs):
    sources, out_ref, downs, sems = refs[:4], *refs[4:]
    copies = fetch([(sources[j], downs.at[j]) for j in range(4)], sems)
    targets, _, per_target, double = rows_ref.shape
    quarter = double // 2
    count, hidden_count = slope_ref.shape
    me = me_ref[0]
    back = jnp.zeros((count, hidden_count), F32)
    for j in range(4):
        grad = rows_ref[:, me ^ j, :, quarter:].reshape(count, quarter)
        copies[j].wait()
        back = back + lax.dot_general(
            grad, downs[j], (((1,), (1,)), ((), ())), preferred_element_type=F32
        )
    out_ref[:, :hidden_count] = hidden_ref[...]
    out_ref[:, hidden_count:] = (back * slope_ref[...]).astype(BF16)


def combine_kernel(share_ref, returned_ref, out_ref):
    targets, quarters, per_target, quarter = returned_ref.shape
    shares = split3(share_ref[...])
    for q in range(quarters):
        rows = returned_ref[:, q].reshape(targets * per_target, quarter)
        mixed = sum(jnp.dot(part, rows, preferred_element_type=F32) for part in shares)
        out_ref[:, q * quarter : (q + 1) * quarter] = mixed.astype(BF16)


def moment_kernel(
    me_ref, rows_ref, a0, a1, a2, a3, up_hbm, down_hbm, out_ref, up_ref, down_ref, sems
):
    copies = fetch([(up_hbm, up_ref), (down_hbm, down_ref)], sems)
    acts = (a0, a1, a2, a3)
    me = me_ref[0]
    features, hidden_count = up_ref.shape
    over_rows = (((0,), (0,)), ((), ()))
    up_grad = jnp.zeros((features, hidden_count), F32)
    down_grad = jnp.zeros((hidden_count, features), F32)
    for j in range(4):
        rows = rows_ref[me ^ j].reshape(acts[j].shape[0], 2 * features)
        up_grad = up_grad + lax.dot_general(
            rows[:, :features],
            acts[j][:, hidden_count:],
            over_rows,
            preferred_element_type=F32,
        )
        down_grad = down_grad + lax.dot_general(
            acts[j][:, :hidden_count],
            rows[:, features:],
            over_rows,
            preferred_element_type=F32,
        )
    rest = 1.0 - MOMENT_DECAY
    for copy in copies:
        copy.wait()
    up = (MOMENT_DECAY * up_ref[...].astype(F32) + rest * up_grad).astype(BF16)
    down = (MOMENT_DECAY * down_ref[...].astype(F32) + rest * down_grad).astype(BF16)
    up = up.reshape(32, 16, hidden_count)
    for j in range(2):
        for c in range(3):
            at = j * 384 + c * 128
            out_ref[j * 32 : (j + 1) * 32, c * 16 : (c + 1) * 16, :] = up[:, :, at : at + 128]
    down = down.reshape(16, 48, features)
    for j in range(4):
        out_ref[64 + j * 16 : 80 + j * 16] = down[:, :, j * 128 : (j + 1) * 128]


def pick_kernel(partner_ref, spread_ref, out_ref):
    def step(slot, carry):
        out_ref[slot] = spread_ref[partner_ref[slot]]
        return carry

    lax.fori_loop(0, out_ref.shape[0], step, 0, unroll=8)


def unpack_kernel(pieces_ref, up_ref, down_ref):
    for j in range(2):
        for c in range(3):
            at = j * 384 + c * 128
            part = pieces_ref[j * 32 : (j + 1) * 32, c * 16 : (c + 1) * 16, :]
            up_ref[:, at : at + 128] = part.reshape(512, 128)
    for j in range(4):
        part = pieces_ref[64 + j * 16 : 80 + j * 16]
        down_ref[:, j * 128 : (j + 1) * 128] = part.reshape(768, 128)


def shape_of(dims, dtype=BF16):
    return jax.ShapeDtypeStruct(dims, dtype)


def body(
    tokens,
    expert_ids,
    route_weight,
    cotangent,
    holder,
    partner,
    up_weight,
    down_weight,
    up_moment,
    down_moment,
):
    plane = lax.axis_index("zh").reshape(1).astype(jnp.int32)
    me = lax.axis_index(DP_AXES).reshape(1).astype(jnp.int32)

    packed = call(pack_kernel, "pack", shape_of((24, 4224)), [VMEM] * 5, 10**6, 4 * 10**5)(
        tokens, cotangent, expert_ids.T, route_weight.T, holder.reshape(1, -1)
    )
    gathered = lax.all_gather(packed, "zh", axis=0, tiled=True)

    up0, down0 = up_weight[0], down_weight[0]
    up2, down2 = lax.ppermute(up0, "yl", FLIP), lax.ppermute(down0, "yl", FLIP)
    up1, down1 = lax.ppermute(up0, "core", FLIP), lax.ppermute(down0, "core", FLIP)
    up3, down3 = lax.ppermute(up2, "core", FLIP), lax.ppermute(down2, "core", FLIP)
    gathered, up1, up2, up3, down1, down2, down3 = lax.optimization_barrier(
        (gathered, up1, up2, up3, down1, down2, down3)
    )
    ups, downs = (up0, up1, up2, up3), (down0, down1, down2, down3)

    outgoing, share = call(
        select_kernel,
        "select",
        (shape_of((16, 4, 16, 1024)), shape_of((192, 256), F32)),
        [SMEM, VMEM],
        10**9,
        4 * 10**6,
    )(plane, gathered)
    rows = lax.all_to_all(outgoing, GROUP_AXES, split_axis=0, concat_axis=0, tiled=True)

    hidden, slope, expert_out = call(
        forward_kernel,
        "forward",
        (shape_of((256, 768)), shape_of((256, 768), F32), shape_of((16, 4, 16, 512))),
        [SMEM, VMEM] + [HBM] * 8,
        16 * 10**8,
        10**7,
        (
            pltpu.VMEM((4, 512, 768), BF16),
            pltpu.VMEM((4, 768, 512), BF16),
            pltpu.SemaphoreType.DMA((8,)),
        ),
    )(me, rows, *ups, *downs)
    acts = call(
        back_kernel,
        "back",
        shape_of((256, 1536)),
        [SMEM, VMEM, VMEM, VMEM] + [HBM] * 4,
        8 * 10**8,
        6 * 10**6,
        (pltpu.VMEM((4, 768, 512), BF16), pltpu.SemaphoreType.DMA((4,))),
    )(me, rows, hidden, slope, *downs)
    acts2 = lax.ppermute(acts, "yl", FLIP)
    acts1 = lax.ppermute(acts, "core", FLIP)

    returned = lax.all_to_all(expert_out, GROUP_AXES, split_axis=0, concat_axis=0, tiled=True)
    turned_rows, returned, acts1 = lax.optimization_barrier(
        (rows.transpose(1, 0, 2, 3), returned, acts1)
    )
    by_feature = lax.all_to_all(turned_rows, DP_AXES, split_axis=0, concat_axis=0, tiled=True)
    acts3 = lax.ppermute(acts2, "core", FLIP)
    partial = call(
        combine_kernel, "combine", shape_of((192, 2048)), [VMEM, VMEM], 6 * 10**8, 2 * 10**6, (), 12
    )(share, returned)
    layer_out = lax.psum_scatter(partial, "zh", scatter_dimension=0, tiled=True)

    pieces = call(
        moment_kernel,
        "moments",
        shape_of((128, 48, 128)),
        [SMEM] + [VMEM] * 5 + [HBM] * 2,
        32 * 10**8,
        9 * 10**6,
        (
            pltpu.VMEM((512, 768), BF16),
            pltpu.VMEM((768, 512), BF16),
            pltpu.SemaphoreType.DMA((2,)),
        ),
    )(me, by_feature, acts, acts1, acts2, acts3, up_moment[0], down_moment[0])


    pieces, layer_out = lax.optimization_barrier((pieces, layer_out))
    spread = lax.all_to_all(pieces, SLOT_AXES, split_axis=0, concat_axis=0, tiled=True)
    chosen = call(
        pick_kernel, "pick", shape_of((128, 48, 128)), [SMEM, VMEM], 0, 3 * 10**6, (), 12
    )(partner, spread)
    landed = lax.all_to_all(chosen, SLOT_AXES, split_axis=0, concat_axis=0, tiled=True)
    new_up, new_down = call(
        unpack_kernel,
        "unpack",
        (shape_of((512, 768)), shape_of((768, 512))),
        [VMEM],
        0,
        3 * 10**6,
        (),
        12,
    )(landed)
    return layer_out, new_up[None], new_down[None]


def solution(mesh):
    wide = Mesh(mesh.devices.reshape(2, 8, 2, 4, 2, 2), AXES)
    return jax.shard_map(
        body,
        mesh=wide,
        in_specs=(
            P(AXES, None),
            P(AXES, None),
            P(AXES, None),
            P(AXES, None),
            P(),
            P(),
            P(SLOT_AXES, DP_AXES, None),
            P(SLOT_AXES, None, DP_AXES),
            P(SLOT_AXES, DP_AXES, None),
            P(SLOT_AXES, None, DP_AXES),
        ),
        out_specs=(
            P(AXES, None),
            P(SLOT_AXES, DP_AXES, None),
            P(SLOT_AXES, None, DP_AXES),
        ),
        check_vma=False,
    )
```
